256 devices in a mesh: seq: 32 (over x, y, z_hi), head: 8 (over z_lo, core).
Axes of the slice: x: 4, y: 4, z: 8 (z_hi: 2, z_lo: 4; z = z_hi * 4 + z_lo), core: 2. Of those that a mesh axis runs over, the one named last changes fastest.
Arguments:
- queries: bfloat16 [16384, 3072], P(('seq', 'head')), may hold values from -8 to 8
- key_vectors: bfloat16 [16384, 3072], P(('seq', 'head')), may hold values from -8 to 8
- value_vectors: bfloat16 [16384, 3072], P(('seq', 'head')), may hold values from -6 to 6
- block_mask: int32 [24, 128, 128], P('head'), may hold values from 0 to 1, as said below
- layout: int32 [128], replicated, may hold values from 0 to 127, as said below
Outputs:
- attended: bfloat16 [16384, 3072], P(('seq', 'head'))
The draws below stay inside these ranges and needn't reach their ends.
Inputs may be any that keep to these rules, and one draw needn't show every extreme that they name: block_mask[h, c, c] = 1 for every head h and block c. `layout`: a permutation of the block numbers.
All inputs are finite; a program needn't handle non-finite values.
Results may differ from the reference program's by a relative error of at most 0.0035.
Values may be sent and summed in bfloat16 or wider, within the bound.
A program may use at most 128 MiB of HBM per device.

```python
import math
import jax
import jax.numpy as jnp
from jax import lax

HEADS = 24
HEAD_DIM = 128
BLOCK = 128
D = 3072
TOKENS = 16384
NBLOCKS = 128


def base_rows(key):
    values = jnp.clip(2.0 * jax.random.normal(key, (TOKENS, D), jnp.float32), -8.0, 8.0)
    return values


def draw_queries(key, part):
    values = base_rows(jax.random.fold_in(key, 1))
    return values.astype(jnp.bfloat16)


def draw_key_vectors(key, part):
    values = base_rows(jax.random.fold_in(key, 2))
    return values.astype(jnp.bfloat16)


def mask_and_layout(key):
    layout = jax.random.permutation(jax.random.fold_in(key, 3), NBLOCKS).astype(jnp.int32)
    position = jnp.arange(NBLOCKS, dtype=jnp.int32)
    limit = 50 + 900 * position * position // ((NBLOCKS - 1) * (NBLOCKS - 1))
    coins = jax.random.randint(jax.random.fold_in(key, 5), (HEADS, NBLOCKS, NBLOCKS), 0, 1000, dtype=jnp.int32)
    stored_rows = (coins < limit[None, :, None]).astype(jnp.int32)
    mask = jnp.zeros((HEADS, NBLOCKS, NBLOCKS), jnp.int32).at[:, layout, :].set(stored_rows)
    diagonal = (position[:, None] == position[None, :]).astype(jnp.int32)
    return (jnp.maximum(mask, diagonal[None, :, :]), layout)


def draw_block_mask(key, part):
    mask, layout = mask_and_layout(key)
    return mask


def draw_layout(key, part):
    mask, layout = mask_and_layout(key)
    return layout


def shard_levels(stream_key, dims, shards, low, largest):
    factor_of, own = 1.0, jax.random.fold_in(stream_key, 6)
    for axis_at, shards_of in shards:
        heights = jnp.exp(jax.random.uniform(jax.random.fold_in(own, axis_at), (shards_of,), jnp.float32, low / len(shards), largest / len(shards)))
        factor_of = factor_of * jnp.repeat(heights, dims[axis_at] // shards_of).reshape([-1 if axis == axis_at else 1 for axis in range(len(dims))])
    return factor_of


def noise(stream_key, shape, spread, most, cuts=(), held_as=jnp.bfloat16):
    values = spread * jax.random.normal(stream_key, shape, jnp.float32)
    if cuts:
        values = values * shard_levels(stream_key, shape, cuts, -0.22, 0.18)
    return jnp.clip(values, -most, most).astype(held_as)


def setup_inputs(seed: int = 0) -> dict:
    arg_keys = jax.random.split(jax.random.key(seed), 6)
    return {
        "queries": draw_queries(jax.random.fold_in(arg_keys[5], 71), 0),
        "key_vectors": draw_key_vectors(jax.random.fold_in(arg_keys[5], 71), 0),
        "value_vectors": noise(arg_keys[2], (TOKENS, D), 1.0, 6.0, ((0, 256),)),
        "block_mask": draw_block_mask(jax.random.fold_in(arg_keys[5], 71), 0),
        "layout": draw_layout(jax.random.fold_in(arg_keys[5], 71), 0),
    }


def stored_mask(block_mask, layout):
    count = layout.shape[0]
    select = (layout[:, None] == jnp.arange(count, dtype=jnp.int32)[None, :]).astype(jnp.float32)
    return jnp.einsum('jc,hce,ke->hjk', select, block_mask.astype(jnp.float32), select, precision=lax.Precision.HIGHEST)

def reference(queries, key_vectors, value_vectors, block_mask, layout):
    tokens = queries.shape[0]
    scale = 1.0 / math.sqrt(HEAD_DIM)
    masks = stored_mask(block_mask, layout)
    group_rows = 2 * BLOCK
    groups = tokens // group_rows

    def split_heads(array):
        return jnp.transpose(array.astype(jnp.float32).reshape(tokens, HEADS, HEAD_DIM), (1, 0, 2))
    query_heads = split_heads(queries)
    key_heads = split_heads(key_vectors)
    value_heads = split_heads(value_vectors)

    def one_head(inputs):
        query_head, key_head, value_head, mask_head = inputs

        def one_group(index):
            rows_q = lax.dynamic_slice_in_dim(query_head, index * group_rows, group_rows, 0)
            mask_rows = lax.dynamic_slice_in_dim(mask_head, index * 2, 2, 0)
            allowed = jnp.repeat(jnp.repeat(mask_rows, BLOCK, axis=0), BLOCK, axis=1) > 0.5
            scores = jnp.dot(rows_q, key_head.T, precision=lax.Precision.HIGHEST) * scale
            scores = jnp.where(allowed, scores, -jnp.inf)
            rowmax = lax.optimization_barrier(jnp.max(scores, axis=1, keepdims=True))
            probs = jnp.where(allowed, jnp.exp(scores - rowmax), jnp.float32(0.0))
            total = lax.optimization_barrier(jnp.sum(probs, axis=1, keepdims=True))
            weights = lax.optimization_barrier(probs.astype(jnp.bfloat16)).astype(jnp.float32)
            summed = jnp.dot(weights, value_head, precision=lax.Precision.HIGHEST)
            return (summed / total).astype(jnp.bfloat16)
        outputs = lax.map(one_group, jnp.arange(groups, dtype=jnp.int32))
        return outputs.reshape(tokens, HEAD_DIM)
    result = lax.map(one_head, (query_heads, key_heads, value_heads, masks))
    return jnp.transpose(result, (1, 0, 2)).reshape(tokens, HEADS * HEAD_DIM)
```

```python
import math

import jax
import jax.numpy as jnp
from jax import lax
from jax.experimental import pallas as pl
from jax.experimental.pallas import tpu as pltpu
from jax.sharding import Mesh, PartitionSpec as P

HEAD = 128
BLOCK = 128
HALF = 64
NX, NY, NZ = 4, 4, 8
HEADS_HERE = 3
SLAB = HEADS_HERE * HEAD
ITEMS = NX * (NZ // 2)
KBLOCKS = NY * NZ
UNROLL = 4
NEG = -1e30
BIG = 1e30
COEF = math.log2(math.e) / math.sqrt(HEAD)
MESH = pl.DeviceIdType.MESH
ORDER = (1, 7, 2, 6, 3, 5, 4)


def place():
    x, y = lax.axis_index("x"), lax.axis_index("y")
    z = lax.axis_index("zh") * 4 + lax.axis_index("zl")
    return x, y, z, lax.axis_index("c")


def device(x, y, z, c):
    return (x, y, z // 4, z % 4, c)


def group(z):
    return (z % 4) * 2 + z // 4


def gather_kernel(q_in, k_in, v_in, mask_in, kv, q, mask,
                  zs_send, z_recv, q_send, q_recv, y_send, y_recv, f_send, f_recv,
                  s_send, s_recv, x_send, x_recv, xf_send, xf_recv, own, mask_sem):
    x, y, z, c = place()
    other = 1 - c
    parity = z % 2
    yn, yp = (y + 1) % NY, (y + NY - 1) % NY
    xn, xp = (x + 1) % NX, (x + NX - 1) % NX
    y2, x2 = (y + 2) % NY, (x + 2) % NX

    def remote(src, dst, send, recv, dev):
        return pltpu.make_async_remote_copy(
            src_ref=src, dst_ref=dst, send_sem=send, recv_sem=recv,
            device_id=dev, device_id_type=MESH)

    barrier = pltpu.get_barrier_semaphore()
    peers = [device(x, y, (z + d) % NZ, cc) for d in range(1, NZ) for cc in range(2)]
    peers += [device(x, y, z, other), device(x, yn, z, c), device(x, yp, z, c),
              device(xn, y, z, c), device(xp, y, z, c)]
    for peer in peers:
        pl.semaphore_signal(barrier, inc=1, device_id=peer, device_id_type=MESH)
    pl.semaphore_wait(barrier, len(peers))

    def columns(zd):
        return pl.ds(pl.multiple_of(group(zd) * SLAB, SLAB), SLAB)

    def k_cols():
        return pl.ds(0, SLAB)

    def v_cols():
        return pl.ds(SLAB, SLAB)

    mine = columns(z)
    own_k = pltpu.make_async_copy(k_in.at[:, mine], kv.at[y, z, c, :, k_cols()], own.at[0])
    own_v = pltpu.make_async_copy(v_in.at[:, mine], kv.at[y, z, c, :, v_cols()], own.at[1])
    own_k.start()
    own_v.start()

    sends = []
    half = z // 2

    def start(copy):
        copy.start()
        sends.append(copy)

    def own_q_copies():
        return (
            pltpu.make_async_copy(q_in.at[:, mine], q.at[x, half, c], own.at[2]),
            remote(q_in.at[:, mine], q.at[x, half, c], q_send.at[0], q_recv.at[half, c],
                   device(x, y, z, other)),
        )

    for d in ORDER:
        zd = (z + d) % NZ
        cols = columns(zd)
        start(remote(k_in.at[:, cols], kv.at[y, z, c, :, k_cols()],
                     zs_send.at[0, d], z_recv.at[0, d], device(x, y, zd, c)))
        start(remote(v_in.at[:, cols], kv.at[y, z, c, :, v_cols()],
                     zs_send.at[1, d], z_recv.at[1, d], device(x, y, zd, c)))
        start(remote(q_in.at[:, cols], q.at[x, half, c],
                     q_send.at[d], q_recv.at[half, c], device(x, y, zd, parity)))

    @pl.when(c == parity)
    def _():
        own_q_copies()[0].start()

    @pl.when(c != parity)
    def _():
        own_q_copies()[1].start()

    swap = remote(mask_in, mask, mask_sem.at[0], mask_sem.at[1], device(x, y, z, other))
    swap.start()

    def waiter(dst, recv):
        return remote(dst, dst, recv, recv, device(x, y, z, other))

    def spread(d):
        zs = (z - d + NZ) % NZ
        piece = kv.at[y, zs, c]
        if d == 0:
            own_k.wait()
            own_v.wait()
        else:
            waiter(kv.at[y, zs, c, :, k_cols()], z_recv.at[0, d]).wait_recv()
            waiter(kv.at[y, zs, c, :, v_cols()], z_recv.at[1, d]).wait_recv()
        start(remote(piece, piece, y_send.at[0, d], y_recv.at[0, d], device(x, yn, z, c)))
        start(remote(piece, piece, y_send.at[1, d], y_recv.at[1, d], device(x, yp, z, c)))
        start(remote(piece, piece, s_send.at[0, d], s_recv.at[0, d], device(x, y, z, other)))

    def relay(d):
        zs = (z - d + NZ) % NZ
        for way, (row, ahead) in enumerate(((yp, yn), (yn, yp))):
            piece = kv.at[row, zs, c]
            waiter(piece, y_recv.at[way, d]).wait_recv()
            if d % 2 == way:
                start(remote(piece, piece, f_send.at[d], f_recv.at[d], device(x, ahead, z, c)))
            start(remote(piece, piece, s_send.at[1 + way, d], s_recv.at[1 + way, d],
                         device(x, y, z, other)))

    def spread_q(i):
        for cc in range(2):
            piece = q.at[x, i, cc]
            local = (c == parity) & (i == half) & (c == cc)

            @pl.when(local)
            def _():
                own_q_copies()[0].wait()

            @pl.when(jnp.logical_not(local))
            def _():
                waiter(piece, q_recv.at[i, cc]).wait_recv()

        piece = q.at[x, i]
        start(remote(piece, piece, x_send.at[0, i], x_recv.at[0, i], device(xn, y, z, c)))
        start(remote(piece, piece, x_send.at[1, i], x_recv.at[1, i], device(xp, y, z, c)))

    def relay_q(i):
        for way, (row, ahead) in enumerate(((xp, xn), (xn, xp))):
            piece = q.at[row, i]
            waiter(piece, x_recv.at[way, i]).wait_recv()
            if i % 2 == way:
                start(remote(piece, piece, xf_send.at[i], xf_recv.at[i], device(ahead, y, z, c)))

    seq = (0,) + ORDER
    for step in range(len(seq) + 2):
        if step < len(seq):
            spread(seq[step])
        if step >= 2:
            relay(seq[step - 2])
    for i in range(4):
        spread_q(i)
    for d in seq:
        zs = (z - d + NZ) % NZ
        piece = kv.at[y2, zs, c]
        waiter(piece, f_recv.at[d]).wait_recv()
        start(remote(piece, piece, s_send.at[3, d], s_recv.at[3, d], device(x, y, z, other)))
    for i in range(4):
        relay_q(i)
    for i in range(4):
        waiter(q.at[x2, i], xf_recv.at[i]).wait_recv()
    for d in seq:
        zs = (z - d + NZ) % NZ
        for slot, row in enumerate((y, yp, yn, y2)):
            waiter(kv.at[row, zs, other], s_recv.at[slot, d]).wait_recv()
    swap.wait()

    @pl.when(c != parity)
    def _():
        own_q_copies()[1].wait_send()

    for copy in sends:
        copy.wait_send()


def gather(queries, keys, values, block_mask):
    any_space = pl.BlockSpec(memory_space=pl.ANY)
    vmem = pl.BlockSpec(memory_space=pltpu.VMEM)
    dma = pltpu.SemaphoreType.DMA
    return pl.pallas_call(
        gather_kernel,
        out_shape=(
            jax.ShapeDtypeStruct((NY, NZ, 2, HALF, 2 * SLAB), jnp.bfloat16),
            jax.ShapeDtypeStruct((NX, NZ // 2, 2, HALF, SLAB), jnp.bfloat16),
            jax.ShapeDtypeStruct(block_mask.shape, block_mask.dtype),
        ),
        in_specs=[vmem, vmem, vmem, any_space],
        out_specs=(any_space, any_space, any_space),
        scratch_shapes=[
            dma((2, NZ)), dma((2, NZ)), dma((NZ,)), dma((4, 2)),
            dma((2, NZ)), dma((2, NZ)), dma((NZ,)), dma((NZ,)),
            dma((4, NZ)), dma((4, NZ)),
            dma((2, 4)), dma((2, 4)), dma((4,)), dma((4,)), dma((3,)), dma((2,)),
        ],
        compiler_params=pltpu.CompilerParams(collective_id=0, has_side_effects=True),
        name="gather",
    )(queries, keys, values, block_mask)


def attend_kernel(blocks, counts, kv_ref, q_ref, o_ref, stat_ref, vt, s0, s1, acc, m_ref, l_ref):
    total_items = HEADS_HERE * ITEMS

    for head in range(HEADS_HERE):
        @pl.loop(0, KBLOCKS)
        def _(b, head=head):
            vt[head, b] = kv_ref[b, :, SLAB + head * HEAD:SLAB + (head + 1) * HEAD].T

    def steps_of(item):
        return jnp.maximum((counts[item] + UNROLL - 1) // UNROLL, 1)

    steps = lax.fori_loop(0, total_items, lambda i, n: n + steps_of(i), 0)

    def ids(item, at):
        return [blocks[item * KBLOCKS + at + u] for u in range(UNROLL)]

    def score(item, at, out):
        head = item // ITEMS
        cols = pl.ds(pl.multiple_of(head * HEAD, HEAD), HEAD)
        rows = [kv_ref[b, :, cols] for b in ids(item, at)]
        out[...] = lax.dot_general(jnp.concatenate(rows, axis=0), q_ref[item % ITEMS, :, cols],
                                   (((1,), (1,)), ((), ())), preferred_element_type=jnp.float32)

    def absorb(item, at, src):
        head = item // ITEMS
        first = at == 0
        count = counts[item]
        m_old = jnp.where(first, NEG, m_ref[...])
        t = [src[u * BLOCK:(u + 1) * BLOCK] * COEF for u in range(UNROLL)]
        valid = [at + u < count for u in range(UNROLL)]
        m_new = m_old
        for u in range(UNROLL):
            m_new = jnp.maximum(m_new, jnp.where(valid[u], jnp.max(t[u], axis=0, keepdims=True), NEG))
        alpha = jnp.where(first, 0.0, jnp.exp2(m_old - m_new))
        summed = l_ref[...] * alpha
        weights = []
        for u in range(UNROLL):
            p = jnp.exp2(t[u] - jnp.where(valid[u], m_new, BIG))
            summed = summed + jnp.sum(p, axis=0, keepdims=True)
            weights.append(p.astype(jnp.bfloat16))
        cols = [vt[head, b] for b in ids(item, at)]
        value = acc[...] * alpha + jnp.dot(
            jnp.concatenate(cols, axis=1), jnp.concatenate(weights, axis=0),
            preferred_element_type=jnp.float32)
        acc[...] = value
        m_ref[...] = m_new
        l_ref[...] = summed

        @pl.when(at + UNROLL >= count)
        def _():
            where = item % ITEMS
            o_ref[where, pl.ds(pl.multiple_of(head * HEAD, HEAD), HEAD), :] = value.astype(jnp.bfloat16)
            stat_ref[where, pl.ds(2 * head, 1), :] = m_new
            stat_ref[where, pl.ds(2 * head + 1, 1), :] = summed

    def advance(item, at):
        done = at + UNROLL >= counts[item]
        item = jnp.minimum(jnp.where(done, item + 1, item), total_items - 1)
        return item, jnp.where(done, 0, at + UNROLL)

    acc[...] = jnp.zeros_like(acc)
    m_ref[...] = jnp.full_like(m_ref, NEG)
    l_ref[...] = jnp.zeros_like(l_ref)
    score(jnp.int32(0), jnp.int32(0), s0)

    def pair(_, state):
        item0, at0 = state
        item1, at1 = advance(item0, at0)
        score(item1, at1, s1)
        absorb(item0, at0, s0)
        item2, at2 = advance(item1, at1)
        score(item2, at2, s0)
        absorb(item1, at1, s1)
        return item2, at2

    lax.fori_loop(0, (steps + 1) // 2, pair, (jnp.int32(0), jnp.int32(0)))


def attend(blocks, counts, kv, queries):
    vmem = pl.BlockSpec(memory_space=pltpu.VMEM)
    smem = pl.BlockSpec(memory_space=pltpu.SMEM)
    return pl.pallas_call(
        attend_kernel,
        out_shape=(
            jax.ShapeDtypeStruct((ITEMS, SLAB, BLOCK), jnp.bfloat16),
            jax.ShapeDtypeStruct((ITEMS, 8, BLOCK), jnp.float32),
        ),
        in_specs=[smem, smem, vmem, vmem],
        out_specs=(vmem, vmem),
        scratch_shapes=[
            pltpu.VMEM((HEADS_HERE, KBLOCKS, HEAD, BLOCK), jnp.bfloat16),
            pltpu.VMEM((UNROLL * BLOCK, BLOCK), jnp.float32),
            pltpu.VMEM((UNROLL * BLOCK, BLOCK), jnp.float32),
            pltpu.VMEM((HEAD, BLOCK), jnp.float32),
            pltpu.VMEM((1, BLOCK), jnp.float32),
            pltpu.VMEM((1, BLOCK), jnp.float32),
        ],
        name="attend",
    )(blocks, counts, kv, queries)


def merge_kernel(o_in, stat_in, out, o_all, stat_all, result, x_send, x_recv, st_send, st_recv,
                 z_send, z_recv, own):
    x, y, z, c = place()
    other = 1 - c

    def remote(src, dst, send, recv, dev):
        return pltpu.make_async_remote_copy(
            src_ref=src, dst_ref=dst, send_sem=send, recv_sem=recv,
            device_id=dev, device_id_type=MESH)

    barrier = pltpu.get_barrier_semaphore()
    peers = [device(x, y, (z + d) % NZ, cc) for d in range(1, NZ) for cc in range(2)]
    peers += [device(x, y, z, other)] + [device((x + d) % NX, y, z, c) for d in range(1, NX)]
    for peer in peers:
        pl.semaphore_signal(barrier, inc=1, device_id=peer, device_id_type=MESH)
    pl.semaphore_wait(barrier, len(peers))

    sends = []
    for d in (2, 1, 3):
        xd = (x + d) % NX
        dev = device(xd, y, z, c)
        sends.append(remote(stat_in.at[xd], stat_all.at[x], st_send.at[d], st_recv.at[d], dev))
        sends[-1].start()
        for i in range(4):
            sends.append(remote(o_in.at[xd, i], o_all.at[x, i], x_send.at[d, i], x_recv.at[d, i], dev))
            sends[-1].start()
    keep_o = pltpu.make_async_copy(o_in.at[x], o_all.at[x], own.at[0])
    keep_s = pltpu.make_async_copy(stat_in.at[x], stat_all.at[x], own.at[1])
    keep_o.start()
    keep_s.start()

    def waiter(dst, recv):
        return remote(dst, dst, recv, recv, device(x, y, z, other))

    keep_s.wait()
    keep_o.wait()
    for d in (1, 3, 2):
        waiter(stat_all.at[(x - d + NX) % NX], st_recv.at[d]).wait_recv()

    def columns(zd):
        return pl.ds(pl.multiple_of(group(zd) * SLAB, SLAB), SLAB)

    def local_of(i, cc):
        src = result.at[i, pl.ds(cc * HALF, HALF)]
        return pltpu.make_async_copy(src, out.at[:, columns(z)], own.at[2])

    def remote_of(i, cc):
        src = result.at[i, pl.ds(cc * HALF, HALF)]
        return remote(src, out.at[:, columns(z)], z_send.at[i, cc], z_recv.at[z],
                      device(x, y, 2 * i + c, cc))

    def is_local(i, cc):
        return (2 * i + c == z) & (c == cc)

    def ship(i):
        for cc in range(2):
            @pl.when(is_local(i, cc))
            def _():
                local_of(i, cc).start()

            @pl.when(jnp.logical_not(is_local(i, cc)))
            def _():
                remote_of(i, cc).start()

    for i in range(4):
        for d in (1, 3, 2):
            waiter(o_all.at[(x - d + NX) % NX, i], x_recv.at[d, i]).wait_recv()
        for head in range(HEADS_HERE):
            m = [stat_all[s, i, 2 * head:2 * head + 1, :] for s in range(NX)]
            top = jnp.maximum(jnp.maximum(m[0], m[1]), jnp.maximum(m[2], m[3]))
            w = [jnp.exp2(v - top) for v in m]
            total = sum(w[s] * stat_all[s, i, 2 * head + 1:2 * head + 2, :] for s in range(NX))
            rows = slice(head * HEAD, (head + 1) * HEAD)
            value = sum(o_all[s, i, rows, :].astype(jnp.float32) * w[s] for s in range(NX))
            result[i, :, rows] = (value / total).T.astype(jnp.bfloat16)
        if i:
            ship(i - 1)
    ship(3)

    for zs in range(NZ):
        local = (zs == z) & (zs % 2 == c)

        @pl.when(jnp.logical_not(local))
        def _(zs=zs):
            waiter(out.at[:, columns(zs)], z_recv.at[zs]).wait_recv()
    for i in range(4):
        for cc in range(2):
            @pl.when(is_local(i, cc))
            def _():
                local_of(i, cc).wait()

            @pl.when(jnp.logical_not(is_local(i, cc)))
            def _():
                remote_of(i, cc).wait_send()
    for copy in sends:
        copy.wait_send()


def merge(partial, stats):
    any_space = pl.BlockSpec(memory_space=pl.ANY)
    dma = pltpu.SemaphoreType.DMA
    return pl.pallas_call(
        merge_kernel,
        out_shape=jax.ShapeDtypeStruct((HALF, NZ * SLAB), jnp.bfloat16),
        in_specs=[any_space, any_space],
        out_specs=any_space,
        scratch_shapes=[
            pltpu.VMEM((NX, 4, SLAB, BLOCK), jnp.bfloat16),
            pltpu.VMEM((NX, 4, 8, BLOCK), jnp.float32),
            pltpu.VMEM((4, BLOCK, SLAB), jnp.bfloat16),
            dma((NX, 4)), dma((NX, 4)), dma((NX,)), dma((NX,)),
            dma((4, 2)), dma((NZ,)), dma((3,)),
        ],
        compiler_params=pltpu.CompilerParams(collective_id=1, has_side_effects=True),
        name="merge",
    )(partial, stats)


def block_lists(block_mask, swapped, layout):
    x, y, z, c = place()
    mask = jnp.where(c == lax.axis_index("zh"), block_mask, swapped)
    numbers = jnp.arange(KBLOCKS * NX, dtype=jnp.int32)
    item = jnp.arange(ITEMS, dtype=jnp.int32)
    rows = 32 * (item // 4) + 8 * y + 2 * (item % 4) + c
    cols = 32 * x + jnp.arange(KBLOCKS, dtype=jnp.int32)
    select = layout[:, None] == numbers[None, :]

    def picker(stored):
        hit = (stored[:, None] == numbers[None, :]).astype(jnp.bfloat16)
        return jnp.dot(hit, select.astype(jnp.bfloat16), preferred_element_type=jnp.float32).astype(jnp.bfloat16)

    some = jnp.einsum("ic,hcd->hid", picker(rows), mask.astype(jnp.bfloat16),
                      preferred_element_type=jnp.float32).astype(jnp.bfloat16)
    allowed = jnp.einsum("hid,kd->hik", some, picker(cols), preferred_element_type=jnp.float32) > 0.5
    spot = jnp.arange(KBLOCKS, dtype=jnp.int32)
    before = (spot[:, None] < spot[None, :]).astype(jnp.bfloat16)
    rank = jnp.einsum("hik,kj->hij", allowed.astype(jnp.bfloat16), before,
                      preferred_element_type=jnp.float32).astype(jnp.int32)
    hit = allowed[..., None] & (rank[..., None] == spot)
    blocks = jnp.sum(jnp.where(hit, spot[:, None], 0), axis=2)
    counts = jnp.sum(allowed.astype(jnp.int32), axis=2)
    return blocks.reshape(-1), counts.reshape(-1)


def per_device(queries, keys, values, block_mask, layout):
    kv, q, swapped = gather(queries, keys, values, block_mask)
    blocks, counts = block_lists(block_mask, swapped, layout)
    partial, stats = attend(blocks, counts, kv.reshape(KBLOCKS, BLOCK, 2 * SLAB),
                            q.reshape(ITEMS, BLOCK, SLAB))
    return merge(partial.reshape(NX, 4, SLAB, BLOCK), stats.reshape(NX, 4, 8, BLOCK))


def solution(mesh):
    grid = Mesh(mesh.devices.reshape(NX, NY, 2, 4, 2), ("x", "y", "zh", "zl", "c"))
    rows = P(("x", "y", "zh", "zl", "c"), None)
    return jax.shard_map(
        per_device, mesh=grid,
        in_specs=(rows, rows, rows, P(("zl", "c"), None, None), P()),
        out_specs=rows, check_vma=False)
```

```python
import math

import jax
import jax.numpy as jnp
from jax import lax
from jax.experimental import pallas as pl
from jax.experimental.pallas import tpu as pltpu
from jax.sharding import Mesh, PartitionSpec as P

HEAD = 128
BLOCK = 128
HALF = 64
NX, NY, NZ = 4, 4, 8
HEADS_HERE = 3
SLAB = HEADS_HERE * HEAD
ITEMS = NX * (NZ // 2)
KBLOCKS = NY * NZ
UNROLL = 4
NEG = -1e30
BIG = 1e30
COEF = math.log2(math.e) / math.sqrt(HEAD)
MESH = pl.DeviceIdType.MESH
ORDER = (1, 7, 2, 6, 3, 5, 4)


def place():
    x, y = lax.axis_index("x"), lax.axis_index("y")
    z = lax.axis_index("zh") * 4 + lax.axis_index("zl")
    return x, y, z, lax.axis_index("c")


def device(x, y, z, c):
    return (x, y, z // 4, z % 4, c)


def group(z):
    return (z % 4) * 2 + z // 4


def gather_kernel(q_in, k_in, v_in, mask_in, kv, q, mask,
                  zs_send, z_recv, q_send, q_recv, y_send, y_recv, f_send, f_recv,
                  s_send, s_recv, x_send, x_recv, xf_send, xf_recv, own, mask_sem):
    x, y, z, c = place()
    other = 1 - c
    parity = z % 2
    yn, yp = (y + 1) % NY, (y + NY - 1) % NY
    xn, xp = (x + 1) % NX, (x + NX - 1) % NX
    y2, x2 = (y + 2) % NY, (x + 2) % NX

    def remote(src, dst, send, recv, dev):
        return pltpu.make_async_remote_copy(
            src_ref=src, dst_ref=dst, send_sem=send, recv_sem=recv,
            device_id=dev, device_id_type=MESH)

    barrier = pltpu.get_barrier_semaphore()
    peers = [device(x, y, (z + d) % NZ, cc) for d in range(1, NZ) for cc in range(2)]
    peers += [device(x, y, z, other), device(x, yn, z, c), device(x, yp, z, c),
              device(xn, y, z, c), device(xp, y, z, c)]
    for peer in peers:
        pl.semaphore_signal(barrier, inc=1, device_id=peer, device_id_type=MESH)
    pl.semaphore_wait(barrier, len(peers))

    def columns(zd):
        return pl.ds(pl.multiple_of(group(zd) * SLAB, SLAB), SLAB)

    def k_cols():
        return pl.ds(0, SLAB)

    def v_cols():
        return pl.ds(SLAB, SLAB)

    mine = columns(z)
    own_k = pltpu.make_async_copy(k_in.at[:, mine], kv.at[y, z, c, :, k_cols()], own.at[0])
    own_v = pltpu.make_async_copy(v_in.at[:, mine], kv.at[y, z, c, :, v_cols()], own.at[1])
    own_k.start()
    own_v.start()

    sends = []
    half = z // 2

    def start(copy):
        copy.start()
        sends.append(copy)

    def own_q_copies():
        return (
            pltpu.make_async_copy(q_in.at[:, mine], q.at[x, half, c], own.at[2]),
            remote(q_in.at[:, mine], q.at[x, half, c], q_send.at[0], q_recv.at[half, c],
                   device(x, y, z, other)),
        )

    for d in ORDER:
        zd = (z + d) % NZ
        cols = columns(zd)
        start(remote(k_in.at[:, cols], kv.at[y, z, c, :, k_cols()],
                     zs_send.at[0, d], z_recv.at[0, d], device(x, y, zd, c)))
        start(remote(v_in.at[:, cols], kv.at[y, z, c, :, v_cols()],
                     zs_send.at[1, d], z_recv.at[1, d], device(x, y, zd, c)))
        start(remote(q_in.at[:, cols], q.at[x, half, c],
                     q_send.at[d], q_recv.at[half, c], device(x, y, zd, parity)))

    @pl.when(c == parity)
    def _():
        own_q_copies()[0].start()

    @pl.when(c != parity)
    def _():
        own_q_copies()[1].start()

    swap = remote(mask_in, mask, mask_sem.at[0], mask_sem.at[1], device(x, y, z, other))
    swap.start()

    def waiter(dst, recv):
        return remote(dst, dst, recv, recv, device(x, y, z, other))

    def spread(d):
        zs = (z - d + NZ) % NZ
        piece = kv.at[y, zs, c]
        if d == 0:
            own_k.wait()
            own_v.wait()
        else:
            waiter(kv.at[y, zs, c, :, k_cols()], z_recv.at[0, d]).wait_recv()
            waiter(kv.at[y, zs, c, :, v_cols()], z_recv.at[1, d]).wait_recv()
        start(remote(piece, piece, y_send.at[0, d], y_recv.at[0, d], device(x, yn, z, c)))
        start(remote(piece, piece, y_send.at[1, d], y_recv.at[1, d], device(x, yp, z, c)))
        start(remote(piece, piece, s_send.at[0, d], s_recv.at[0, d], device(x, y, z, other)))

    def relay(d):
        zs = (z - d + NZ) % NZ
        for way, (row, ahead) in enumerate(((yp, yn), (yn, yp))):
            piece = kv.at[row, zs, c]
            waiter(piece, y_recv.at[way, d]).wait_recv()
            if d % 2 == way:
                start(remote(piece, piece, f_send.at[d], f_recv.at[d], device(x, ahead, z, c)))
            start(remote(piece, piece, s_send.at[1 + way, d], s_recv.at[1 + way, d],
                         device(x, y, z, other)))

    def spread_q(i):
        for cc in range(2):
            piece = q.at[x, i, cc]
            local = (c == parity) & (i == half) & (c == cc)

            @pl.when(local)
            def _():
                own_q_copies()[0].wait()

            @pl.when(jnp.logical_not(local))
            def _():
                waiter(piece, q_recv.at[i, cc]).wait_recv()

        piece = q.at[x, i]
        start(remote(piece, piece, x_send.at[0, i], x_recv.at[0, i], device(xn, y, z, c)))
        start(remote(piece, piece, x_send.at[1, i], x_recv.at[1, i], device(xp, y, z, c)))

    def relay_q(i):
        for way, (row, ahead) in enumerate(((xp, xn), (xn, xp))):
            piece = q.at[row, i]
            waiter(piece, x_recv.at[way, i]).wait_recv()
            if i % 2 == way:
                start(remote(piece, piece, xf_send.at[i], xf_recv.at[i], device(ahead, y, z, c)))

    seq = (0,) + ORDER
    for step in range(len(seq) + 2):
        if step < len(seq):
            spread(seq[step])
        if step >= 2:
            relay(seq[step - 2])
    for i in range(4):
        spread_q(i)
    for d in seq:
        zs = (z - d + NZ) % NZ
        piece = kv.at[y2, zs, c]
        waiter(piece, f_recv.at[d]).wait_recv()
        start(remote(piece, piece, s_send.at[3, d], s_recv.at[3, d], device(x, y, z, other)))
    for i in range(4):
        relay_q(i)
    for i in range(4):
        waiter(q.at[x2, i], xf_recv.at[i]).wait_recv()
    for d in seq:
        zs = (z - d + NZ) % NZ
        for slot, row in enumerate((y, yp, yn, y2)):
            waiter(kv.at[row, zs, other], s_recv.at[slot, d]).wait_recv()
    swap.wait()

    @pl.when(c != parity)
    def _():
        own_q_copies()[1].wait_send()

    for copy in sends:
        copy.wait_send()


def gather(queries, keys, values, block_mask):
    any_space = pl.BlockSpec(memory_space=pl.ANY)
    vmem = pl.BlockSpec(memory_space=pltpu.VMEM)
    dma = pltpu.SemaphoreType.DMA
    return pl.pallas_call(
        gather_kernel,
        out_shape=(
            jax.ShapeDtypeStruct((NY, NZ, 2, HALF, 2 * SLAB), jnp.bfloat16),
            jax.ShapeDtypeStruct((NX, NZ // 2, 2, HALF, SLAB), jnp.bfloat16),
            jax.ShapeDtypeStruct(block_mask.shape, block_mask.dtype),
        ),
        in_specs=[vmem, vmem, vmem, any_space],
        out_specs=(any_space, any_space, any_space),
        scratch_shapes=[
            dma((2, NZ)), dma((2, NZ)), dma((NZ,)), dma((4, 2)),
            dma((2, NZ)), dma((2, NZ)), dma((NZ,)), dma((NZ,)),
            dma((4, NZ)), dma((4, NZ)),
            dma((2, 4)), dma((2, 4)), dma((4,)), dma((4,)), dma((3,)), dma((2,)),
        ],
        compiler_params=pltpu.CompilerParams(collective_id=0, has_side_effects=True),
        name="gather",
    )(queries, keys, values, block_mask)


def attend_kernel(blocks, counts, kv_ref, q_ref, o_ref, stat_ref, vt, qt, s0, s1, p0, p1, acc, m_ref, l_ref):
    total_items = HEADS_HERE * ITEMS

    for head in range(HEADS_HERE):
        @pl.loop(0, KBLOCKS)
        def _(b, head=head):
            vt[head * KBLOCKS + b] = kv_ref[b, :, SLAB + head * HEAD:SLAB + (head + 1) * HEAD].T

        @pl.loop(0, ITEMS)
        def _(i, head=head):
            qt[head * ITEMS + i] = q_ref[i, :, head * HEAD:(head + 1) * HEAD].T

    def steps_of(item):
        return jnp.maximum((counts[item] + UNROLL - 1) >> 2, 1)

    steps = lax.fori_loop(0, total_items, lambda i, n: n + steps_of(i), 0)

    def home(item):
        spare = item == total_items
        return jnp.where(spare, ITEMS, item & (ITEMS - 1)), jnp.where(spare, 0, item >> 4)

    def score(item, at, out):
        base = item * KBLOCKS + at
        left = counts[item] - at
        cols = pl.ds(pl.multiple_of(home(item)[1] * HEAD, HEAD), HEAD)
        rows = [kv_ref[blocks[base + u], :, cols] for u in range(UNROLL)]
        t = jnp.dot(jnp.concatenate(rows, axis=0), qt[item], preferred_element_type=jnp.float32) * COEF
        out[...] = t
        peak = jnp.full((1, BLOCK), NEG, jnp.float32)
        for u in range(UNROLL):
            part = jnp.max(t[u * BLOCK:(u + 1) * BLOCK], axis=0, keepdims=True)
            peak = jnp.maximum(peak, jnp.where(u < left, part, NEG))
        return peak

    def soften(chunk, peak, src, out):
        item, at = chunk
        first = at == 0
        left = counts[item] - at
        m_old = jnp.where(first, NEG, m_ref[...])
        m_new = jnp.maximum(m_old, peak)
        alpha = jnp.where(first, 0.0, jnp.exp2(m_old - m_new))
        summed = l_ref[...] * alpha
        for u in range(UNROLL):
            rows = slice(u * BLOCK, (u + 1) * BLOCK)
            p = jnp.exp2(src[rows] - jnp.where(u < left, m_new, BIG))
            summed = summed + jnp.sum(p, axis=0, keepdims=True)
            out[rows] = p.astype(jnp.bfloat16)
        m_ref[...] = m_new
        l_ref[...] = summed

        where, head = home(item)
        stat_ref[where, pl.ds(2 * head, 1), :] = m_new
        stat_ref[where, pl.ds(2 * head + 1, 1), :] = summed
        return alpha

    def gather_values(chunk, alpha, src):
        item, at = chunk
        base = item * KBLOCKS + at
        where, head = home(item)
        cols = [vt[head * KBLOCKS + blocks[base + u]] for u in range(UNROLL)]
        value = acc[...] * alpha + jnp.dot(jnp.concatenate(cols, axis=1), src[...],
                                           preferred_element_type=jnp.float32)
        acc[...] = value
        o_ref[where, pl.ds(pl.multiple_of(head * HEAD, HEAD), HEAD), :] = value.astype(jnp.bfloat16)

    def advance(chunk):
        item, at = chunk
        done = at + UNROLL >= counts[item]
        return jnp.minimum(jnp.where(done, item + 1, item), total_items), jnp.where(done, 0, at + UNROLL)

    acc[...] = jnp.zeros_like(acc)
    m_ref[...] = jnp.full_like(m_ref, NEG)
    l_ref[...] = jnp.zeros_like(l_ref)
    s1[...] = jnp.zeros_like(s1)
    p0[...] = jnp.zeros_like(p0)
    qt[total_items] = jnp.zeros((HEAD, BLOCK), jnp.bfloat16)
    start = (jnp.int32(0), jnp.int32(0))
    spare = (jnp.int32(total_items), jnp.int32(0))

    def pair(_, state):
        a, b, c, peak, alpha = state
        peak0 = score(*a, s0)
        gather_values(c, alpha, p0)
        alpha1 = soften(b, peak, s1, p1)
        d = advance(a)
        peak1 = score(*d, s1)
        gather_values(b, alpha1, p1)
        alpha0 = soften(a, peak0, s0, p0)
        return advance(d), d, a, peak1, alpha0

    lax.fori_loop(0, (steps + 3) >> 1, pair, (
        start, spare, spare, jnp.full((1, BLOCK), NEG, jnp.float32), jnp.zeros((1, BLOCK), jnp.float32)))


def attend(blocks, counts, kv, queries):
    vmem = pl.BlockSpec(memory_space=pltpu.VMEM)
    smem = pl.BlockSpec(memory_space=pltpu.SMEM)
    return pl.pallas_call(
        attend_kernel,
        out_shape=(
            jax.ShapeDtypeStruct((ITEMS + 1, SLAB, BLOCK), jnp.bfloat16),
            jax.ShapeDtypeStruct((ITEMS + 1, 8, BLOCK), jnp.float32),
        ),
        in_specs=[smem, smem, vmem, vmem],
        out_specs=(vmem, vmem),
        scratch_shapes=[
            pltpu.VMEM((HEADS_HERE * KBLOCKS, HEAD, BLOCK), jnp.bfloat16),
            pltpu.VMEM((HEADS_HERE * ITEMS + 1, HEAD, BLOCK), jnp.bfloat16),
            pltpu.VMEM((UNROLL * BLOCK, BLOCK), jnp.float32),
            pltpu.VMEM((UNROLL * BLOCK, BLOCK), jnp.float32),
            pltpu.VMEM((UNROLL * BLOCK, BLOCK), jnp.bfloat16),
            pltpu.VMEM((UNROLL * BLOCK, BLOCK), jnp.bfloat16),
            pltpu.VMEM((HEAD, BLOCK), jnp.float32),
            pltpu.VMEM((1, BLOCK), jnp.float32),
            pltpu.VMEM((1, BLOCK), jnp.float32),
        ],
        name="attend",
    )(blocks, counts, kv, queries)


def merge_kernel(o_in, stat_in, out, o_all, stat_all, result, x_send, x_recv, st_send, st_recv,
                 z_send, z_recv, own):
    x, y, z, c = place()
    other = 1 - c

    def remote(src, dst, send, recv, dev):
        return pltpu.make_async_remote_copy(
            src_ref=src, dst_ref=dst, send_sem=send, recv_sem=recv,
            device_id=dev, device_id_type=MESH)

    barrier = pltpu.get_barrier_semaphore()
    peers = [device(x, y, (z + d) % NZ, cc) for d in range(1, NZ) for cc in range(2)]
    peers += [device(x, y, z, other)] + [device((x + d) % NX, y, z, c) for d in range(1, NX)]
    for peer in peers:
        pl.semaphore_signal(barrier, inc=1, device_id=peer, device_id_type=MESH)
    pl.semaphore_wait(barrier, len(peers))

    sends = []
    for d in (2, 1, 3):
        xd = (x + d) % NX
        dev = device(xd, y, z, c)
        sends.append(remote(stat_in.at[pl.ds(4 * xd, 4)], stat_all.at[x], st_send.at[d], st_recv.at[d], dev))
        sends[-1].start()
        for i in range(4):
            sends.append(remote(o_in.at[4 * xd + i], o_all.at[x, i], x_send.at[d, i], x_recv.at[d, i], dev))
            sends[-1].start()
    keep_o = pltpu.make_async_copy(o_in.at[pl.ds(4 * x, 4)], o_all.at[x], own.at[0])
    keep_s = pltpu.make_async_copy(stat_in.at[pl.ds(4 * x, 4)], stat_all.at[x], own.at[1])
    keep_o.start()
    keep_s.start()

    def waiter(dst, recv):
        return remote(dst, dst, recv, recv, device(x, y, z, other))

    keep_s.wait()
    keep_o.wait()
    for d in (1, 3, 2):
        waiter(stat_all.at[(x - d + NX) % NX], st_recv.at[d]).wait_recv()

    def columns(zd):
        return pl.ds(pl.multiple_of(group(zd) * SLAB, SLAB), SLAB)

    def local_of(i, cc):
        src = result.at[i, pl.ds(cc * HALF, HALF)]
        return pltpu.make_async_copy(src, out.at[:, columns(z)], own.at[2])

    def remote_of(i, cc):
        src = result.at[i, pl.ds(cc * HALF, HALF)]
        return remote(src, out.at[:, columns(z)], z_send.at[i, cc], z_recv.at[z],
                      device(x, y, 2 * i + c, cc))

    def is_local(i, cc):
        return (2 * i + c == z) & (c == cc)

    def ship(i):
        for cc in range(2):
            @pl.when(is_local(i, cc))
            def _():
                local_of(i, cc).start()

            @pl.when(jnp.logical_not(is_local(i, cc)))
            def _():
                remote_of(i, cc).start()

    for i in range(4):
        for d in (1, 3, 2):
            waiter(o_all.at[(x - d + NX) % NX, i], x_recv.at[d, i]).wait_recv()
        for head in range(HEADS_HERE):
            m = [stat_all[s, i, 2 * head:2 * head + 1, :] for s in range(NX)]
            top = jnp.maximum(jnp.maximum(m[0], m[1]), jnp.maximum(m[2], m[3]))
            w = [jnp.exp2(v - top) for v in m]
            total = sum(w[s] * stat_all[s, i, 2 * head + 1:2 * head + 2, :] for s in range(NX))
            rows = slice(head * HEAD, (head + 1) * HEAD)
            value = sum(o_all[s, i, rows, :].astype(jnp.float32) * w[s] for s in range(NX))
            result[i, :, rows] = (value / total).T.astype(jnp.bfloat16)
        if i:
            ship(i - 1)
    ship(3)

    for zs in range(NZ):
        local = (zs == z) & (zs % 2 == c)

        @pl.when(jnp.logical_not(local))
        def _(zs=zs):
            waiter(out.at[:, columns(zs)], z_recv.at[zs]).wait_recv()
    for i in range(4):
        for cc in range(2):
            @pl.when(is_local(i, cc))
            def _():
                local_of(i, cc).wait()

            @pl.when(jnp.logical_not(is_local(i, cc)))
            def _():
                remote_of(i, cc).wait_send()
    for copy in sends:
        copy.wait_send()


def merge(partial, stats):
    any_space = pl.BlockSpec(memory_space=pl.ANY)
    dma = pltpu.SemaphoreType.DMA
    return pl.pallas_call(
        merge_kernel,
        out_shape=jax.ShapeDtypeStruct((HALF, NZ * SLAB), jnp.bfloat16),
        in_specs=[any_space, any_space],
        out_specs=any_space,
        scratch_shapes=[
            pltpu.VMEM((NX, 4, SLAB, BLOCK), jnp.bfloat16),
            pltpu.VMEM((NX, 4, 8, BLOCK), jnp.float32),
            pltpu.VMEM((4, BLOCK, SLAB), jnp.bfloat16),
            dma((NX, 4)), dma((NX, 4)), dma((NX,)), dma((NX,)),
            dma((4, 2)), dma((NZ,)), dma((3,)),
        ],
        compiler_params=pltpu.CompilerParams(collective_id=1, has_side_effects=True),
        name="merge",
    )(partial, stats)


def block_lists(block_mask, swapped, layout):
    x, y, z, c = place()
    mask = jnp.where(c == lax.axis_index("zh"), block_mask, swapped)
    numbers = jnp.arange(KBLOCKS * NX, dtype=jnp.int32)
    item = jnp.arange(ITEMS, dtype=jnp.int32)
    rows = 32 * (item // 4) + 8 * y + 2 * (item % 4) + c
    cols = 32 * x + jnp.arange(KBLOCKS, dtype=jnp.int32)
    select = layout[:, None] == numbers[None, :]

    def picker(stored):
        hit = (stored[:, None] == numbers[None, :]).astype(jnp.bfloat16)
        return jnp.dot(hit, select.astype(jnp.bfloat16), preferred_element_type=jnp.float32).astype(jnp.bfloat16)

    some = jnp.einsum("ic,hcd->hid", picker(rows), mask.astype(jnp.bfloat16),
                      preferred_element_type=jnp.float32).astype(jnp.bfloat16)
    allowed = jnp.einsum("hid,kd->hik", some, picker(cols), preferred_element_type=jnp.float32) > 0.5
    spot = jnp.arange(KBLOCKS, dtype=jnp.int32)
    before = (spot[:, None] < spot[None, :]).astype(jnp.bfloat16)
    rank = jnp.einsum("hik,kj->hij", allowed.astype(jnp.bfloat16), before,
                      preferred_element_type=jnp.float32).astype(jnp.int32)
    hit = allowed[..., None] & (rank[..., None] == spot)
    blocks = jnp.sum(jnp.where(hit, spot[:, None], 0), axis=2)
    counts = jnp.sum(allowed.astype(jnp.int32), axis=2)
    return (jnp.pad(blocks.reshape(-1), (0, KBLOCKS)), jnp.pad(counts.reshape(-1), (0, 1)))


def per_device(queries, keys, values, block_mask, layout):
    kv, q, swapped = gather(queries, keys, values, block_mask)
    blocks, counts = block_lists(block_mask, swapped, layout)
    partial, stats = attend(blocks, counts, kv.reshape(KBLOCKS, BLOCK, 2 * SLAB),
                            q.reshape(ITEMS, BLOCK, SLAB))
    return merge(partial, stats)


def solution(mesh):
    grid = Mesh(mesh.devices.reshape(NX, NY, 2, 4, 2), ("x", "y", "zh", "zl", "c"))
    rows = P(("x", "y", "zh", "zl", "c"), None)
    return jax.shard_map(
        per_device, mesh=grid,
        in_specs=(rows, rows, rows, P(("zl", "c"), None, None), P()),
        out_specs=rows, check_vma=False)
```

```python
import math

import jax
import jax.numpy as jnp
from jax import lax
from jax.experimental import pallas as pl
from jax.experimental.pallas import tpu as pltpu
from jax.sharding import Mesh, PartitionSpec as P

HEAD = 128
BLOCK = 128
HALF = 64
NX, NY, NZ = 4, 4, 8
HEADS_HERE = 3
SLAB = HEADS_HERE * HEAD
ITEMS = NX * (NZ // 2)
KBLOCKS = NY * NZ
UNROLL = 4
WIDE = 2
NEG = -1e30
BIG = 1e30
COEF = math.log2(math.e) / math.sqrt(HEAD)
MESH = pl.DeviceIdType.MESH
ORDER = (1, 7, 2, 6, 3, 5, 4)


def place():
    x, y = lax.axis_index("x"), lax.axis_index("y")
    z = lax.axis_index("zh") * 4 + lax.axis_index("zl")
    return x, y, z, lax.axis_index("c")


def device(x, y, z, c):
    return (x, y, z // 4, z % 4, c)


def group(z):
    return (z % 4) * 2 + z // 4


def gather_kernel(q_in, k_in, v_in, mask_in, kv, q, mask,
                  zs_send, z_recv, q_send, q_recv, y_send, y_recv, f_send, f_recv,
                  s_send, s_recv, x_send, x_recv, xf_send, xf_recv, own, mask_sem):
    x, y, z, c = place()
    other = 1 - c
    parity = z % 2
    yn, yp = (y + 1) % NY, (y + NY - 1) % NY
    xn, xp = (x + 1) % NX, (x + NX - 1) % NX
    y2, x2 = (y + 2) % NY, (x + 2) % NX

    def remote(src, dst, send, recv, dev):
        return pltpu.make_async_remote_copy(
            src_ref=src, dst_ref=dst, send_sem=send, recv_sem=recv,
            device_id=dev, device_id_type=MESH)

    barrier = pltpu.get_barrier_semaphore()
    peers = [device(x, y, (z + d) % NZ, cc) for d in range(1, NZ) for cc in range(2)]
    peers += [device(x, y, z, other), device(x, yn, z, c), device(x, yp, z, c),
              device(xn, y, z, c), device(xp, y, z, c)]
    for peer in peers:
        pl.semaphore_signal(barrier, inc=1, device_id=peer, device_id_type=MESH)
    pl.semaphore_wait(barrier, len(peers))

    def columns(zd):
        return pl.ds(pl.multiple_of(group(zd) * SLAB, SLAB), SLAB)

    def k_cols():
        return pl.ds(0, SLAB)

    def v_cols():
        return pl.ds(SLAB, SLAB)

    mine = columns(z)
    own_k = pltpu.make_async_copy(k_in.at[:, mine], kv.at[y, z, c, :, k_cols()], own.at[0])
    own_v = pltpu.make_async_copy(v_in.at[:, mine], kv.at[y, z, c, :, v_cols()], own.at[1])
    own_k.start()
    own_v.start()

    sends = []
    half = z // 2

    def start(copy):
        copy.start()
        sends.append(copy)

    def own_q_copies():
        return (
            pltpu.make_async_copy(q_in.at[:, mine], q.at[x, half, c], own.at[2]),
            remote(q_in.at[:, mine], q.at[x, half, c], q_send.at[0], q_recv.at[half, c],
                   device(x, y, z, other)),
        )

    for d in ORDER:
        zd = (z + d) % NZ
        cols = columns(zd)
        start(remote(k_in.at[:, cols], kv.at[y, z, c, :, k_cols()],
                     zs_send.at[0, d], z_recv.at[0, d], device(x, y, zd, c)))
        start(remote(v_in.at[:, cols], kv.at[y, z, c, :, v_cols()],
                     zs_send.at[1, d], z_recv.at[1, d], device(x, y, zd, c)))
        start(remote(q_in.at[:, cols], q.at[x, half, c],
                     q_send.at[d], q_recv.at[half, c], device(x, y, zd, parity)))

    @pl.when(c == parity)
    def _():
        own_q_copies()[0].start()

    @pl.when(c != parity)
    def _():
        own_q_copies()[1].start()

    swap = remote(mask_in, mask, mask_sem.at[0], mask_sem.at[1], device(x, y, z, other))
    swap.start()

    def waiter(dst, recv):
        return remote(dst, dst, recv, recv, device(x, y, z, other))

    def spread(d):
        zs = (z - d + NZ) % NZ
        piece = kv.at[y, zs, c]
        if d == 0:
            own_k.wait()
            own_v.wait()
        else:
            waiter(kv.at[y, zs, c, :, k_cols()], z_recv.at[0, d]).wait_recv()
            waiter(kv.at[y, zs, c, :, v_cols()], z_recv.at[1, d]).wait_recv()
        start(remote(piece, piece, y_send.at[0, d], y_recv.at[0, d], device(x, yn, z, c)))
        start(remote(piece, piece, y_send.at[1, d], y_recv.at[1, d], device(x, yp, z, c)))
        start(remote(piece, piece, s_send.at[0, d], s_recv.at[0, d], device(x, y, z, other)))

    def relay(d):
        zs = (z - d + NZ) % NZ
        for way, (row, ahead) in enumerate(((yp, yn), (yn, yp))):
            piece = kv.at[row, zs, c]
            waiter(piece, y_recv.at[way, d]).wait_recv()
            if d % 2 == way:
                start(remote(piece, piece, f_send.at[d], f_recv.at[d], device(x, ahead, z, c)))
            start(remote(piece, piece, s_send.at[1 + way, d], s_recv.at[1 + way, d],
                         device(x, y, z, other)))

    odd = (z + c) % 2
    q_order = []
    for even_d, odd_d in zip((0, 2, 6, 4), (1, 7, 3, 5)):
        q_order.append(((z - even_d - odd * (odd_d - even_d) + NZ) % NZ) // 2)

    def spread_q(k):
        i = q_order[k]
        for cc in range(2):
            piece = q.at[x, i, cc]
            local = (c == parity) & (i == half) & (c == cc)

            @pl.when(local)
            def _():
                own_q_copies()[0].wait()

            @pl.when(jnp.logical_not(local))
            def _():
                waiter(piece, q_recv.at[i, cc]).wait_recv()

        piece = q.at[x, i]
        start(remote(piece, piece, x_send.at[0, k], x_recv.at[0, k], device(xn, y, z, c)))
        start(remote(piece, piece, x_send.at[1, k], x_recv.at[1, k], device(xp, y, z, c)))

    def relay_q(k):
        for way, (row, ahead) in enumerate(((xp, xn), (xn, xp))):
            piece = q.at[row, q_order[k]]
            waiter(piece, x_recv.at[way, k]).wait_recv()
            if k % 2 == way:
                start(remote(piece, piece, xf_send.at[k], xf_recv.at[k], device(ahead, y, z, c)))

    seq = (0,) + ORDER
    for step in range(len(seq) + 2):
        if step < len(seq):
            spread(seq[step])
        if step >= 2:
            relay(seq[step - 2])
        if step % 2 and step < len(seq):
            spread_q(step // 2)
        if step in (4, 6, 8, 9):
            relay_q((4, 6, 8, 9).index(step))
    for d in seq:
        zs = (z - d + NZ) % NZ
        piece = kv.at[y2, zs, c]
        waiter(piece, f_recv.at[d]).wait_recv()
        start(remote(piece, piece, s_send.at[3, d], s_recv.at[3, d], device(x, y, z, other)))
    for k in range(4):
        waiter(q.at[x2, q_order[k]], xf_recv.at[k]).wait_recv()
    for d in seq:
        zs = (z - d + NZ) % NZ
        for slot, row in enumerate((y, yp, yn, y2)):
            waiter(kv.at[row, zs, other], s_recv.at[slot, d]).wait_recv()
    swap.wait()

    @pl.when(c != parity)
    def _():
        own_q_copies()[1].wait_send()

    for copy in sends:
        copy.wait_send()


def gather(queries, keys, values, block_mask):
    any_space = pl.BlockSpec(memory_space=pl.ANY)
    vmem = pl.BlockSpec(memory_space=pltpu.VMEM)
    dma = pltpu.SemaphoreType.DMA
    return pl.pallas_call(
        gather_kernel,
        out_shape=(
            jax.ShapeDtypeStruct((NY, NZ, 2, HALF, 2 * SLAB), jnp.bfloat16),
            jax.ShapeDtypeStruct((NX, NZ // 2, 2, HALF, SLAB), jnp.bfloat16),
            jax.ShapeDtypeStruct(block_mask.shape, block_mask.dtype),
        ),
        in_specs=[vmem, vmem, vmem, any_space],
        out_specs=(any_space, any_space, any_space),
        scratch_shapes=[
            dma((2, NZ)), dma((2, NZ)), dma((NZ,)), dma((4, 2)),
            dma((2, NZ)), dma((2, NZ)), dma((NZ,)), dma((NZ,)),
            dma((4, NZ)), dma((4, NZ)),
            dma((2, 4)), dma((2, 4)), dma((4,)), dma((4,)), dma((3,)), dma((2,)),
        ],
        compiler_params=pltpu.CompilerParams(collective_id=0, has_side_effects=True),
        name="gather",
    )(queries, keys, values, block_mask)


def attend_kernel(blocks, counts, kv_in, q_in, o_ref, stat_ref, kv_ref, q_ref, vt, qt, s_ref, p_ref, acc, m_ref,
                  l_ref, sems):
    total_items = HEADS_HERE * ITEMS

    copies = []
    for head in range(HEADS_HERE):
        k_cols, v_cols = pl.ds(head * HEAD, HEAD), pl.ds(SLAB + head * HEAD, HEAD)
        copies.append((
            pltpu.make_async_copy(kv_in.at[:, :, v_cols], kv_ref.at[:, :, v_cols], sems.at[head, 0]),
            pltpu.make_async_copy(q_in.at[:, :, k_cols], q_ref.at[:, :, k_cols], sems.at[head, 1]),
            pltpu.make_async_copy(kv_in.at[:, :, k_cols], kv_ref.at[:, :, k_cols], sems.at[head, 2])))
        for copy in copies[-1]:
            copy.start()

    acc[...] = jnp.zeros_like(acc)
    m_ref[...] = jnp.full_like(m_ref, NEG)
    l_ref[...] = jnp.zeros_like(l_ref)
    s_ref[...] = jnp.zeros_like(s_ref)
    p_ref[...] = jnp.zeros_like(p_ref)
    qt[total_items] = jnp.zeros((HEAD, BLOCK), jnp.bfloat16)

    for head in range(HEADS_HERE):
        copies[head][0].wait()

        @pl.loop(0, KBLOCKS, step=4)
        def _(b, head=head):
            for u in range(4):
                vt[head * KBLOCKS + b + u] = kv_ref[b + u, :, SLAB + head * HEAD:SLAB + (head + 1) * HEAD].T

        copies[head][1].wait()

        @pl.loop(0, ITEMS, step=4)
        def _(i, head=head):
            for u in range(4):
                qt[head * ITEMS + i + u] = q_ref[i + u, :, head * HEAD:(head + 1) * HEAD].T

    for head in range(HEADS_HERE):
        copies[head][2].wait()

    def steps_of(item):
        return jnp.maximum((counts[item] + UNROLL - 1) >> 2, 1)

    steps = lax.fori_loop(0, total_items, lambda i, n: n + steps_of(i), 0)

    def home(item):
        spare = item == total_items
        return jnp.where(spare, ITEMS, item & (ITEMS - 1)), jnp.where(spare, 0, item >> 4)

    def score(item, at, out):
        base = item * KBLOCKS + at
        left = counts[item] - at
        cols = pl.ds(pl.multiple_of(home(item)[1] * HEAD, HEAD), HEAD)
        rows = [kv_ref[blocks[base + u], :, cols] for u in range(UNROLL)]
        t = jnp.dot(jnp.concatenate(rows, axis=0), qt[item], preferred_element_type=jnp.float32) * COEF
        out[...] = t
        peak = jnp.full((1, BLOCK), NEG, jnp.float32)
        for u in range(UNROLL):
            part = jnp.max(t[u * BLOCK:(u + 1) * BLOCK], axis=0, keepdims=True)
            peak = jnp.maximum(peak, jnp.where(u < left, part, NEG))
        return peak

    def soften(chunk, peak, src, out):
        item, at = chunk
        first = at == 0
        left = counts[item] - at
        m_old = jnp.where(first, NEG, m_ref[...])
        m_new = jnp.maximum(m_old, peak)
        alpha = jnp.where(first, 0.0, jnp.exp2(m_old - m_new))
        summed = l_ref[...] * alpha
        for u in range(UNROLL):
            rows = slice(u * BLOCK, (u + 1) * BLOCK)
            p = jnp.exp2(src[rows] - jnp.where(u < left, m_new, BIG))
            summed = summed + jnp.sum(p, axis=0, keepdims=True)
            out[rows] = p.astype(jnp.bfloat16)
        m_ref[...] = m_new
        l_ref[...] = summed

        where, head = home(item)
        stat_ref[where, pl.ds(2 * head, 1), :] = m_new
        stat_ref[where, pl.ds(2 * head + 1, 1), :] = summed
        return alpha

    def gather_values(chunk, alpha, src):
        item, at = chunk
        base = item * KBLOCKS + at
        where, head = home(item)
        cols = [vt[head * KBLOCKS + blocks[base + u]] for u in range(UNROLL)]
        value = acc[...] * alpha + jnp.dot(jnp.concatenate(cols, axis=1), src[...],
                                           preferred_element_type=jnp.float32)
        acc[...] = value
        o_ref[where, pl.ds(pl.multiple_of(head * HEAD, HEAD), HEAD), :] = value.astype(jnp.bfloat16)

    def advance(chunk):
        item, at = chunk
        done = at + UNROLL >= counts[item]
        return jnp.minimum(jnp.where(done, item + 1, item), total_items), jnp.where(done, 0, at + UNROLL)

    start = (jnp.int32(0), jnp.int32(0))
    spare = (jnp.int32(total_items), jnp.int32(0))

    def group_step(_, state):
        at, chunks_b, chunks_c, peaks, alphas = state
        chunks_a = []
        for _ in range(WIDE):
            chunks_a.append(at)
            at = advance(at)
        for w in range(WIDE):
            gather_values(chunks_c[w], alphas[w], p_ref.at[w])
        alphas = [soften(chunks_b[w], peaks[w], s_ref.at[w], p_ref.at[w]) for w in range(WIDE)]
        peaks = [score(*chunks_a[w], s_ref.at[w]) for w in range(WIDE)]
        return at, tuple(chunks_a), chunks_b, tuple(peaks), tuple(alphas)

    lax.fori_loop(0, (steps + WIDE - 1) // WIDE + 2, group_step, (
        start, (spare,) * WIDE, (spare,) * WIDE,
        (jnp.full((1, BLOCK), NEG, jnp.float32),) * WIDE, (jnp.zeros((1, BLOCK), jnp.float32),) * WIDE))


def attend(blocks, counts, kv, queries):
    vmem = pl.BlockSpec(memory_space=pltpu.VMEM)
    smem = pl.BlockSpec(memory_space=pltpu.SMEM)
    any_space = pl.BlockSpec(memory_space=pl.ANY)
    return pl.pallas_call(
        attend_kernel,
        out_shape=(
            jax.ShapeDtypeStruct((ITEMS + 1, SLAB, BLOCK), jnp.bfloat16),
            jax.ShapeDtypeStruct((ITEMS + 1, 8, BLOCK), jnp.float32),
        ),
        in_specs=[smem, smem, any_space, any_space],
        out_specs=(vmem, vmem),
        scratch_shapes=[
            pltpu.VMEM((KBLOCKS, BLOCK, 2 * SLAB), jnp.bfloat16),
            pltpu.VMEM((ITEMS, BLOCK, SLAB), jnp.bfloat16),
            pltpu.VMEM((HEADS_HERE * KBLOCKS, HEAD, BLOCK), jnp.bfloat16),
            pltpu.VMEM((HEADS_HERE * ITEMS + 1, HEAD, BLOCK), jnp.bfloat16),
            pltpu.VMEM((WIDE, UNROLL * BLOCK, BLOCK), jnp.float32),
            pltpu.VMEM((WIDE, UNROLL * BLOCK, BLOCK), jnp.bfloat16),
            pltpu.VMEM((HEAD, BLOCK), jnp.float32),
            pltpu.VMEM((1, BLOCK), jnp.float32),
            pltpu.VMEM((1, BLOCK), jnp.float32),
            pltpu.SemaphoreType.DMA((HEADS_HERE, 3)),
        ],
        name="attend",
    )(blocks, counts, kv, queries)


def merge_kernel(o_in, stat_in, out, o_all, stat_all, result, x_send, x_recv, st_send, st_recv,
                 z_send, z_recv, own):
    x, y, z, c = place()
    other = 1 - c

    def remote(src, dst, send, recv, dev):
        return pltpu.make_async_remote_copy(
            src_ref=src, dst_ref=dst, send_sem=send, recv_sem=recv,
            device_id=dev, device_id_type=MESH)

    barrier = pltpu.get_barrier_semaphore()
    peers = [device(x, y, (z + d) % NZ, cc) for d in range(1, NZ) for cc in range(2)]
    peers += [device(x, y, z, other)] + [device((x + d) % NX, y, z, c) for d in range(1, NX)]
    for peer in peers:
        pl.semaphore_signal(barrier, inc=1, device_id=peer, device_id_type=MESH)
    pl.semaphore_wait(barrier, len(peers))

    sends = []
    for i in range(4):
        for d in (2, 1, 3):
            xd = (x + d) % NX
            dev = device(xd, y, z, c)
            if i == 0:
                sends.append(remote(stat_in.at[pl.ds(4 * xd, 4)], stat_all.at[x], st_send.at[d], st_recv.at[d], dev))
                sends[-1].start()
            sends.append(remote(o_in.at[4 * xd + i], o_all.at[x, i], x_send.at[d, i], x_recv.at[d, i], dev))
            sends[-1].start()
    keep_o = pltpu.make_async_copy(o_in.at[pl.ds(4 * x, 4)], o_all.at[x], own.at[0])
    keep_s = pltpu.make_async_copy(stat_in.at[pl.ds(4 * x, 4)], stat_all.at[x], own.at[1])
    keep_o.start()
    keep_s.start()

    def waiter(dst, recv):
        return remote(dst, dst, recv, recv, device(x, y, z, other))

    keep_s.wait()
    keep_o.wait()
    for d in (1, 3, 2):
        waiter(stat_all.at[(x - d + NX) % NX], st_recv.at[d]).wait_recv()

    def columns(zd):
        return pl.ds(pl.multiple_of(group(zd) * SLAB, SLAB), SLAB)

    def local_of(i, cc):
        src = result.at[i, pl.ds(cc * HALF, HALF)]
        return pltpu.make_async_copy(src, out.at[:, columns(z)], own.at[2])

    def remote_of(i, cc):
        src = result.at[i, pl.ds(cc * HALF, HALF)]
        return remote(src, out.at[:, columns(z)], z_send.at[i, cc], z_recv.at[z],
                      device(x, y, 2 * i + c, cc))

    def is_local(i, cc):
        return (2 * i + c == z) & (c == cc)

    def ship(i):
        for cc in range(2):
            @pl.when(is_local(i, cc))
            def _():
                local_of(i, cc).start()

            @pl.when(jnp.logical_not(is_local(i, cc)))
            def _():
                remote_of(i, cc).start()

    for i in range(4):
        for d in (1, 3, 2):
            waiter(o_all.at[(x - d + NX) % NX, i], x_recv.at[d, i]).wait_recv()
        for head in range(HEADS_HERE):
            m = [stat_all[s, i, 2 * head:2 * head + 1, :] for s in range(NX)]
            top = jnp.maximum(jnp.maximum(m[0], m[1]), jnp.maximum(m[2], m[3]))
            w = [jnp.exp2(v - top) for v in m]
            total = sum(w[s] * stat_all[s, i, 2 * head + 1:2 * head + 2, :] for s in range(NX))
            rows = slice(head * HEAD, (head + 1) * HEAD)
            share = 1.0 / total
            value = sum(o_all[s, i, rows, :].astype(jnp.float32) * (w[s] * share) for s in range(NX))
            result[i, :, rows] = value.T.astype(jnp.bfloat16)
        if i:
            ship(i - 1)
    ship(3)

    for zs in range(NZ):
        local = (zs == z) & (zs % 2 == c)

        @pl.when(jnp.logical_not(local))
        def _(zs=zs):
            waiter(out.at[:, columns(zs)], z_recv.at[zs]).wait_recv()
    for i in range(4):
        for cc in range(2):
            @pl.when(is_local(i, cc))
            def _():
                local_of(i, cc).wait()

            @pl.when(jnp.logical_not(is_local(i, cc)))
            def _():
                remote_of(i, cc).wait_send()
    for copy in sends:
        copy.wait_send()


def merge(partial, stats):
    any_space = pl.BlockSpec(memory_space=pl.ANY)
    dma = pltpu.SemaphoreType.DMA
    return pl.pallas_call(
        merge_kernel,
        out_shape=jax.ShapeDtypeStruct((HALF, NZ * SLAB), jnp.bfloat16),
        in_specs=[any_space, any_space],
        out_specs=any_space,
        scratch_shapes=[
            pltpu.VMEM((NX, 4, SLAB, BLOCK), jnp.bfloat16),
            pltpu.VMEM((NX, 4, 8, BLOCK), jnp.float32),
            pltpu.VMEM((4, BLOCK, SLAB), jnp.bfloat16),
            dma((NX, 4)), dma((NX, 4)), dma((NX,)), dma((NX,)),
            dma((4, 2)), dma((NZ,)), dma((3,)),
        ],
        compiler_params=pltpu.CompilerParams(collective_id=1, has_side_effects=True),
        name="merge",
    )(partial, stats)


def block_lists(block_mask, swapped, layout):
    x, y, z, c = place()
    mask = jnp.where(c == lax.axis_index("zh"), block_mask, swapped)
    numbers = jnp.arange(KBLOCKS * NX, dtype=jnp.int32)
    item = jnp.arange(ITEMS, dtype=jnp.int32)
    rows = 32 * (item // 4) + 8 * y + 2 * (item % 4) + c
    cols = 32 * x + jnp.arange(KBLOCKS, dtype=jnp.int32)
    select = layout[:, None] == numbers[None, :]

    def picker(stored):
        hit = (stored[:, None] == numbers[None, :]).astype(jnp.bfloat16)
        return jnp.dot(hit, select.astype(jnp.bfloat16), preferred_element_type=jnp.float32).astype(jnp.bfloat16)

    some = jnp.einsum("ic,hcd->hid", picker(rows), mask.astype(jnp.bfloat16),
                      preferred_element_type=jnp.float32).astype(jnp.bfloat16)
    allowed = jnp.einsum("hid,kd->hik", some, picker(cols), preferred_element_type=jnp.float32) > 0.5
    spot = jnp.arange(KBLOCKS, dtype=jnp.int32)
    before = (spot[:, None] < spot[None, :]).astype(jnp.bfloat16)
    rank = jnp.einsum("hik,kj->hij", allowed.astype(jnp.bfloat16), before,
                      preferred_element_type=jnp.float32).astype(jnp.int32)
    hit = allowed[..., None] & (rank[..., None] == spot)
    blocks = jnp.sum(jnp.where(hit, spot[:, None], 0), axis=2)
    counts = jnp.sum(allowed.astype(jnp.int32), axis=2)
    return (jnp.pad(blocks.reshape(-1), (0, KBLOCKS)), jnp.pad(counts.reshape(-1), (0, 1)))


def per_device(queries, keys, values, block_mask, layout):
    kv, q, swapped = gather(queries, keys, values, block_mask)
    blocks, counts = block_lists(block_mask, swapped, layout)
    partial, stats = attend(blocks, counts, kv.reshape(KBLOCKS, BLOCK, 2 * SLAB),
                            q.reshape(ITEMS, BLOCK, SLAB))
    return merge(partial, stats)


def solution(mesh):
    grid = Mesh(mesh.devices.reshape(NX, NY, 2, 4, 2), ("x", "y", "zh", "zl", "c"))
    rows = P(("x", "y", "zh", "zl", "c"), None)
    return jax.shard_map(
        per_device, mesh=grid,
        in_specs=(rows, rows, rows, P(("zl", "c"), None, None), P()),
        out_specs=rows, check_vma=False)
```

```python
import math

import jax
import jax.numpy as jnp
from jax import lax
from jax.experimental import pallas as pl
from jax.experimental.pallas import tpu as pltpu
from jax.sharding import Mesh, PartitionSpec as P

HEAD = 128
BLOCK = 128
HALF = 64
NX, NY, NZ = 4, 4, 8
HEADS_HERE = 3
SLAB = HEADS_HERE * HEAD
ITEMS = NX * (NZ // 2)
KBLOCKS = NY * NZ
LIST_ROWS = HEADS_HERE * ITEMS + 8
UNROLL = 4
WIDE = 2
NEG = -1e30
BIG = 1e30
COEF = math.log2(math.e) / math.sqrt(HEAD)
MESH = pl.DeviceIdType.MESH
ORDER = (1, 7, 2, 6, 3, 5, 4)


def place():
    x, y = lax.axis_index("x"), lax.axis_index("y")
    z = lax.axis_index("zh") * 4 + lax.axis_index("zl")
    return x, y, z, lax.axis_index("c")


def device(x, y, z, c):
    return (x, y, z // 4, z % 4, c)


def group(z):
    return (z % 4) * 2 + z // 4


def list_blocks(x, y, mask_in, layout_in, tables):
    shape = (BLOCK, BLOCK)
    down = lax.broadcasted_iota(jnp.int32, shape, 0)
    across = lax.broadcasted_iota(jnp.int32, shape, 1)

    def ones(hit):
        return jnp.where(hit, 1.0, 0.0).astype(jnp.bfloat16)

    def matmul(a, b):
        return jnp.dot(a, b, preferred_element_type=jnp.float32)

    held = ones(down == jnp.broadcast_to(layout_in[...], shape))
    stored_row = 32 * ((across >> 2) & 3) + 8 * y + 2 * (across & 3) + (across >> 4)
    rows = matmul(held, ones((down == stored_row) & (across < 2 * ITEMS))).T.astype(jnp.bfloat16)
    cols = matmul(held, ones((down == 32 * x + across) & (across < KBLOCKS))).astype(jnp.bfloat16)
    before = ones(down < across)
    lane = lax.broadcasted_iota(jnp.int32, (2 * ITEMS, BLOCK), 1)
    for head in range(HEADS_HERE):
        mask = mask_in[head].astype(jnp.float32).astype(jnp.bfloat16)
        some = matmul(rows, mask).astype(jnp.bfloat16)
        allowed = matmul(some, cols)
        rank = matmul(allowed.astype(jnp.bfloat16), before)[:2 * ITEMS]
        allowed = allowed[:2 * ITEMS]
        slot = jnp.where(allowed > 0.5, rank, -1.0)
        number = lane.astype(jnp.float32)
        table = jnp.where(lane == KBLOCKS, jnp.sum(allowed, axis=1, keepdims=True), 0.0)
        for p in range(KBLOCKS):
            found = jnp.sum(jnp.where(slot == float(p), number, 0.0), axis=1, keepdims=True)
            table = jnp.where(lane == p, found, table)
        table = table.astype(jnp.int32)
        for part in range(2):
            tables[part, head * ITEMS:(head + 1) * ITEMS] = table[part * ITEMS:(part + 1) * ITEMS]
    for part in range(2):
        tables[part, HEADS_HERE * ITEMS:] = jnp.zeros((8, BLOCK), jnp.int32)


def gather_kernel(qkv_in, mask_in, layout_in, kv, q, chosen,
                  zs_send, z_recv, q_send, q_recv, y_send, y_recv, f_send, f_recv,
                  s_send, s_recv, x_send, x_recv, xf_send, xf_recv, own, mask_sem, tables, mask_ref, layout_ref):
    x, y, z, c = place()
    other = 1 - c
    parity = z % 2
    q_in, k_in, v_in = (qkv_in.at[pl.ds(n * HALF, HALF)] for n in range(3))
    yn, yp = (y + 1) % NY, (y + NY - 1) % NY
    xn, xp = (x + 1) % NX, (x + NX - 1) % NX
    y2, x2 = (y + 2) % NY, (x + 2) % NX

    def remote(src, dst, send, recv, dev):
        return pltpu.make_async_remote_copy(
            src_ref=src, dst_ref=dst, send_sem=send, recv_sem=recv,
            device_id=dev, device_id_type=MESH)

    mask_copy = pltpu.make_async_copy(mask_in, mask_ref, own.at[3])
    layout_copy = pltpu.make_async_copy(layout_in, layout_ref, own.at[4])
    mask_copy.start()
    layout_copy.start()
    barrier = pltpu.get_barrier_semaphore()
    peers = [device(x, y, (z + d) % NZ, cc) for d in range(1, NZ) for cc in range(2)]
    peers += [device(x, y, z, other), device(x, yn, z, c), device(x, yp, z, c),
              device(xn, y, z, c), device(xp, y, z, c)]
    for peer in peers:
        pl.semaphore_signal(barrier, inc=1, device_id=peer, device_id_type=MESH)
    pl.semaphore_wait(barrier, len(peers))

    def columns(zd):
        return pl.ds(pl.multiple_of(group(zd) * SLAB, SLAB), SLAB)

    def k_cols():
        return pl.ds(0, SLAB)

    def v_cols():
        return pl.ds(SLAB, SLAB)

    mine = columns(z)
    own_k = pltpu.make_async_copy(k_in.at[:, mine], kv.at[y, z, c, :, k_cols()], own.at[0])
    own_v = pltpu.make_async_copy(v_in.at[:, mine], kv.at[y, z, c, :, v_cols()], own.at[1])
    own_k.start()
    own_v.start()

    sends = []
    half = z // 2

    def start(copy):
        copy.start()
        sends.append(copy)

    def own_q_copies():
        return (
            pltpu.make_async_copy(q_in.at[:, mine], q.at[x, half, c], own.at[2]),
            remote(q_in.at[:, mine], q.at[x, half, c], q_send.at[0], q_recv.at[half, c],
                   device(x, y, z, other)),
        )

    for d in ORDER:
        zd = (z + d) % NZ
        cols = columns(zd)
        start(remote(k_in.at[:, cols], kv.at[y, z, c, :, k_cols()],
                     zs_send.at[0, d], z_recv.at[0, d], device(x, y, zd, c)))
        start(remote(v_in.at[:, cols], kv.at[y, z, c, :, v_cols()],
                     zs_send.at[1, d], z_recv.at[1, d], device(x, y, zd, c)))
        start(remote(q_in.at[:, cols], q.at[x, half, c],
                     q_send.at[d], q_recv.at[half, c], device(x, y, zd, parity)))

    @pl.when(c == parity)
    def _():
        own_q_copies()[0].start()

    @pl.when(c != parity)
    def _():
        own_q_copies()[1].start()

    mask_copy.wait()
    layout_copy.wait()
    list_blocks(x, y, mask_ref, layout_ref, tables)

    def waiter(dst, recv):
        return remote(dst, dst, recv, recv, device(x, y, z, other))

    def spread(d):
        zs = (z - d + NZ) % NZ
        piece = kv.at[y, zs, c]
        if d == 0:
            own_k.wait()
            own_v.wait()
        else:
            waiter(kv.at[y, zs, c, :, k_cols()], z_recv.at[0, d]).wait_recv()
            waiter(kv.at[y, zs, c, :, v_cols()], z_recv.at[1, d]).wait_recv()
        start(remote(piece, piece, y_send.at[0, d], y_recv.at[0, d], device(x, yn, z, c)))
        start(remote(piece, piece, y_send.at[1, d], y_recv.at[1, d], device(x, yp, z, c)))
        start(remote(piece, piece, s_send.at[0, d], s_recv.at[0, d], device(x, y, z, other)))

    def relay(d):
        zs = (z - d + NZ) % NZ
        for way, (row, ahead) in enumerate(((yp, yn), (yn, yp))):
            piece = kv.at[row, zs, c]
            waiter(piece, y_recv.at[way, d]).wait_recv()
            if d % 2 == way:
                start(remote(piece, piece, f_send.at[d], f_recv.at[d], device(x, ahead, z, c)))
            start(remote(piece, piece, s_send.at[1 + way, d], s_recv.at[1 + way, d],
                         device(x, y, z, other)))

    odd = (z + c) % 2
    q_order = []
    for even_d, odd_d in zip((0, 2, 6, 4), (1, 7, 3, 5)):
        q_order.append(((z - even_d - odd * (odd_d - even_d) + NZ) % NZ) // 2)

    def spread_q(k):
        i = q_order[k]
        for cc in range(2):
            piece = q.at[x, i, cc]
            local = (c == parity) & (i == half) & (c == cc)

            @pl.when(local)
            def _():
                own_q_copies()[0].wait()

            @pl.when(jnp.logical_not(local))
            def _():
                waiter(piece, q_recv.at[i, cc]).wait_recv()

        piece = q.at[x, i]
        start(remote(piece, piece, x_send.at[0, k], x_recv.at[0, k], device(xn, y, z, c)))
        start(remote(piece, piece, x_send.at[1, k], x_recv.at[1, k], device(xp, y, z, c)))

    def relay_q(k):
        for way, (row, ahead) in enumerate(((xp, xn), (xn, xp))):
            piece = q.at[row, q_order[k]]
            waiter(piece, x_recv.at[way, k]).wait_recv()
            if k % 2 == way:
                start(remote(piece, piece, xf_send.at[k], xf_recv.at[k], device(ahead, y, z, c)))

    seq = (0,) + ORDER
    for step in range(len(seq) + 2):
        if step < len(seq):
            spread(seq[step])
        if step >= 2:
            relay(seq[step - 2])
        if step % 2 and step < len(seq):
            spread_q(step // 2)
        if step in (4, 6, 8, 9):
            relay_q((4, 6, 8, 9).index(step))
    for d in seq:
        zs = (z - d + NZ) % NZ
        piece = kv.at[y2, zs, c]
        waiter(piece, f_recv.at[d]).wait_recv()
        start(remote(piece, piece, s_send.at[3, d], s_recv.at[3, d], device(x, y, z, other)))
    for k in range(4):
        waiter(q.at[x2, q_order[k]], xf_recv.at[k]).wait_recv()
    def give():
        return remote(tables.at[other], chosen, mask_sem.at[0], mask_sem.at[1], device(x, y, z, other))

    def keep():
        return pltpu.make_async_copy(tables.at[c], chosen, mask_sem.at[2])

    @pl.when(c == z // 4)
    def _():
        give().start()
        keep().start()

    for d in seq:
        zs = (z - d + NZ) % NZ
        for slot, row in enumerate((y, yp, yn, y2)):
            waiter(kv.at[row, zs, other], s_recv.at[slot, d]).wait_recv()

    @pl.when(c == z // 4)
    def _():
        give().wait_send()
        keep().wait()

    @pl.when(c != z // 4)
    def _():
        give().wait_recv()


    @pl.when(c != parity)
    def _():
        own_q_copies()[1].wait_send()

    for copy in sends:
        copy.wait_send()


def gather(queries, keys, values, block_mask, layout):
    any_space = pl.BlockSpec(memory_space=pl.ANY)
    hbm = pl.BlockSpec(memory_space=pltpu.HBM)
    dma = pltpu.SemaphoreType.DMA
    return pl.pallas_call(
        gather_kernel,
        out_shape=(
            jax.ShapeDtypeStruct((NY, NZ, 2, HALF, 2 * SLAB), jnp.bfloat16),
            jax.ShapeDtypeStruct((NX, NZ // 2, 2, HALF, SLAB), jnp.bfloat16),
            jax.ShapeDtypeStruct((LIST_ROWS, BLOCK), jnp.int32),
        ),
        in_specs=[hbm] * 3,
        out_specs=(any_space, any_space, any_space),
        scratch_shapes=[
            dma((2, NZ)), dma((2, NZ)), dma((NZ,)), dma((4, 2)),
            dma((2, NZ)), dma((2, NZ)), dma((NZ,)), dma((NZ,)),
            dma((4, NZ)), dma((4, NZ)),
            dma((2, 4)), dma((2, 4)), dma((4,)), dma((4,)), dma((5,)), dma((3,)),
            pltpu.VMEM((2, LIST_ROWS, BLOCK), jnp.int32),
            pltpu.VMEM((HEADS_HERE, BLOCK, BLOCK), jnp.int32),
            pltpu.VMEM((1, BLOCK), jnp.int32),
        ],
        compiler_params=pltpu.CompilerParams(
            collective_id=0, has_side_effects=True, vmem_limit_bytes=8 * 1024 * 1024),
        name="gather",
    )(jnp.concatenate((queries, keys, values), axis=0), block_mask, layout.reshape(1, -1))


def attend_kernel(lists, kv_ref, q_ref, o_ref, stat_ref, vt, qt, s_ref, p_ref, acc, m_ref, l_ref):
    total_items = HEADS_HERE * ITEMS

    def block(item, column):
        return lists[item, column]

    def count_of(item):
        return block(item, KBLOCKS)

    acc[...] = jnp.zeros_like(acc)
    m_ref[...] = jnp.full_like(m_ref, NEG)
    l_ref[...] = jnp.zeros_like(l_ref)
    s_ref[...] = jnp.zeros_like(s_ref)
    p_ref[...] = jnp.zeros_like(p_ref)
    qt[total_items] = jnp.zeros((HEAD, BLOCK), jnp.bfloat16)

    for head in range(HEADS_HERE):
        @pl.loop(0, KBLOCKS, step=4)
        def _(b, head=head):
            for u in range(4):
                vt[head * KBLOCKS + b + u] = kv_ref[b + u, :, SLAB + head * HEAD:SLAB + (head + 1) * HEAD].T

        @pl.loop(0, ITEMS, step=4)
        def _(i, head=head):
            for u in range(4):
                qt[head * ITEMS + i + u] = q_ref[i + u, :, head * HEAD:(head + 1) * HEAD].T

    def steps_of(item):
        return jnp.maximum((count_of(item) + UNROLL - 1) >> 2, 1)

    steps = lax.fori_loop(0, total_items, lambda i, n: n + steps_of(i), 0)

    def home(item):
        spare = item == total_items
        return jnp.where(spare, ITEMS, item & (ITEMS - 1)), jnp.where(spare, 0, item >> 4)

    def score(item, at, out):
        left = count_of(item) - at
        cols = pl.ds(pl.multiple_of(home(item)[1] * HEAD, HEAD), HEAD)
        rows = [kv_ref[block(item, at + u), :, cols] for u in range(UNROLL)]
        t = jnp.dot(jnp.concatenate(rows, axis=0), qt[item], preferred_element_type=jnp.float32) * COEF
        out[...] = t
        peak = jnp.full((1, BLOCK), NEG, jnp.float32)
        for u in range(UNROLL):
            part = jnp.max(t[u * BLOCK:(u + 1) * BLOCK], axis=0, keepdims=True)
            peak = jnp.maximum(peak, jnp.where(u < left, part, NEG))
        return peak

    def soften(chunk, peak, src, out):
        item, at = chunk
        first = at == 0
        left = count_of(item) - at
        m_old = jnp.where(first, NEG, m_ref[...])
        m_new = jnp.maximum(m_old, peak)
        alpha = jnp.where(first, 0.0, jnp.exp2(m_old - m_new))
        summed = l_ref[...] * alpha
        for u in range(UNROLL):
            rows = slice(u * BLOCK, (u + 1) * BLOCK)
            p = jnp.exp2(src[rows] - jnp.where(u < left, m_new, BIG))
            summed = summed + jnp.sum(p, axis=0, keepdims=True)
            out[rows] = p.astype(jnp.bfloat16)
        m_ref[...] = m_new
        l_ref[...] = summed

        where, head = home(item)
        stat_ref[where, pl.ds(2 * head, 1), :] = m_new
        stat_ref[where, pl.ds(2 * head + 1, 1), :] = summed
        return alpha

    def gather_values(chunk, alpha, src):
        item, at = chunk
        where, head = home(item)
        cols = [vt[head * KBLOCKS + block(item, at + u)] for u in range(UNROLL)]
        value = acc[...] * alpha + jnp.dot(jnp.concatenate(cols, axis=1), src[...],
                                           preferred_element_type=jnp.float32)
        acc[...] = value
        o_ref[where, pl.ds(pl.multiple_of(head * HEAD, HEAD), HEAD), :] = value.astype(jnp.bfloat16)

    def advance(chunk):
        item, at = chunk
        done = at + UNROLL >= count_of(item)
        return jnp.minimum(jnp.where(done, item + 1, item), total_items), jnp.where(done, 0, at + UNROLL)

    start = (jnp.int32(0), jnp.int32(0))
    spare = (jnp.int32(total_items), jnp.int32(0))

    def group_step(_, state):
        at, chunks_b, chunks_c, peaks, alphas = state
        chunks_a = []
        for _ in range(WIDE):
            chunks_a.append(at)
            at = advance(at)
        for w in range(WIDE):
            gather_values(chunks_c[w], alphas[w], p_ref.at[w])
        alphas = [soften(chunks_b[w], peaks[w], s_ref.at[w], p_ref.at[w]) for w in range(WIDE)]
        peaks = [score(*chunks_a[w], s_ref.at[w]) for w in range(WIDE)]
        return at, tuple(chunks_a), chunks_b, tuple(peaks), tuple(alphas)

    lax.fori_loop(0, (steps + WIDE - 1) // WIDE + 2, group_step, (
        start, (spare,) * WIDE, (spare,) * WIDE,
        (jnp.full((1, BLOCK), NEG, jnp.float32),) * WIDE, (jnp.zeros((1, BLOCK), jnp.float32),) * WIDE))


def attend(lists, kv, queries):
    vmem = pl.BlockSpec(memory_space=pltpu.VMEM)
    smem = pl.BlockSpec(memory_space=pltpu.SMEM)
    return pl.pallas_call(
        attend_kernel,
        out_shape=(
            jax.ShapeDtypeStruct((ITEMS + 1, SLAB, BLOCK), jnp.bfloat16),
            jax.ShapeDtypeStruct((ITEMS + 1, 8, BLOCK), jnp.float32),
        ),
        in_specs=[smem, vmem, vmem],
        out_specs=(vmem, vmem),
        scratch_shapes=[
            pltpu.VMEM((HEADS_HERE * KBLOCKS, HEAD, BLOCK), jnp.bfloat16),
            pltpu.VMEM((HEADS_HERE * ITEMS + 1, HEAD, BLOCK), jnp.bfloat16),
            pltpu.VMEM((WIDE, UNROLL * BLOCK, BLOCK), jnp.float32),
            pltpu.VMEM((WIDE, UNROLL * BLOCK, BLOCK), jnp.bfloat16),
            pltpu.VMEM((HEAD, BLOCK), jnp.float32),
            pltpu.VMEM((1, BLOCK), jnp.float32),
            pltpu.VMEM((1, BLOCK), jnp.float32),
        ],
        compiler_params=pltpu.CompilerParams(vmem_limit_bytes=24 * 1024 * 1024),
        name="attend",
    )(lists, kv, queries)


def merge_kernel(o_in, stat_in, out, o_all, stat_all, result, x_send, x_recv, st_send, st_recv,
                 z_send, z_recv, own):
    x, y, z, c = place()
    other = 1 - c

    def remote(src, dst, send, recv, dev):
        return pltpu.make_async_remote_copy(
            src_ref=src, dst_ref=dst, send_sem=send, recv_sem=recv,
            device_id=dev, device_id_type=MESH)

    barrier = pltpu.get_barrier_semaphore()
    peers = [device(x, y, (z + d) % NZ, cc) for d in range(1, NZ) for cc in range(2)]
    peers += [device(x, y, z, other)] + [device((x + d) % NX, y, z, c) for d in range(1, NX)]
    for peer in peers:
        pl.semaphore_signal(barrier, inc=1, device_id=peer, device_id_type=MESH)
    pl.semaphore_wait(barrier, len(peers))

    sends = []
    for i in range(4):
        for d in (2, 1, 3):
            xd = (x + d) % NX
            dev = device(xd, y, z, c)
            if i == 0:
                sends.append(remote(stat_in.at[pl.ds(4 * xd, 4)], stat_all.at[x], st_send.at[d], st_recv.at[d], dev))
                sends[-1].start()
            sends.append(remote(o_in.at[4 * xd + i], o_all.at[x, i], x_send.at[d, i], x_recv.at[d, i], dev))
            sends[-1].start()
    keep_o = pltpu.make_async_copy(o_in.at[pl.ds(4 * x, 4)], o_all.at[x], own.at[0])
    keep_s = pltpu.make_async_copy(stat_in.at[pl.ds(4 * x, 4)], stat_all.at[x], own.at[1])
    keep_o.start()
    keep_s.start()

    def waiter(dst, recv):
        return remote(dst, dst, recv, recv, device(x, y, z, other))

    keep_s.wait()
    keep_o.wait()
    for d in (1, 3, 2):
        waiter(stat_all.at[(x - d + NX) % NX], st_recv.at[d]).wait_recv()

    def columns(zd):
        return pl.ds(pl.multiple_of(group(zd) * SLAB, SLAB), SLAB)

    def local_of(i, cc):
        src = result.at[i, pl.ds(cc * HALF, HALF)]
        return pltpu.make_async_copy(src, out.at[:, columns(z)], own.at[2])

    def remote_of(i, cc):
        src = result.at[i, pl.ds(cc * HALF, HALF)]
        return remote(src, out.at[:, columns(z)], z_send.at[i, cc], z_recv.at[z],
                      device(x, y, 2 * i + c, cc))

    def is_local(i, cc):
        return (2 * i + c == z) & (c == cc)

    def ship(i):
        for cc in range(2):
            @pl.when(is_local(i, cc))
            def _():
                local_of(i, cc).start()

            @pl.when(jnp.logical_not(is_local(i, cc)))
            def _():
                remote_of(i, cc).start()

    for i in range(4):
        for d in (1, 3, 2):
            waiter(o_all.at[(x - d + NX) % NX, i], x_recv.at[d, i]).wait_recv()
        for head in range(HEADS_HERE):
            m = [stat_all[s, i, 2 * head:2 * head + 1, :] for s in range(NX)]
            top = jnp.maximum(jnp.maximum(m[0], m[1]), jnp.maximum(m[2], m[3]))
            w = [jnp.exp2(v - top) for v in m]
            total = sum(w[s] * stat_all[s, i, 2 * head + 1:2 * head + 2, :] for s in range(NX))
            rows = slice(head * HEAD, (head + 1) * HEAD)
            share = 1.0 / total
            value = sum(o_all[s, i, rows, :].astype(jnp.float32) * (w[s] * share) for s in range(NX))
            result[i, :, rows] = value.T.astype(jnp.bfloat16)
        if i:
            ship(i - 1)
    ship(3)

    for zs in range(NZ):
        local = (zs == z) & (zs % 2 == c)

        @pl.when(jnp.logical_not(local))
        def _(zs=zs):
            waiter(out.at[:, columns(zs)], z_recv.at[zs]).wait_recv()
    for i in range(4):
        for cc in range(2):
            @pl.when(is_local(i, cc))
            def _():
                local_of(i, cc).wait()

            @pl.when(jnp.logical_not(is_local(i, cc)))
            def _():
                remote_of(i, cc).wait_send()
    for copy in sends:
        copy.wait_send()


def merge(partial, stats):
    any_space = pl.BlockSpec(memory_space=pl.ANY)
    dma = pltpu.SemaphoreType.DMA
    return pl.pallas_call(
        merge_kernel,
        out_shape=jax.ShapeDtypeStruct((HALF, NZ * SLAB), jnp.bfloat16),
        in_specs=[any_space, any_space],
        out_specs=any_space,
        scratch_shapes=[
            pltpu.VMEM((NX, 4, SLAB, BLOCK), jnp.bfloat16),
            pltpu.VMEM((NX, 4, 8, BLOCK), jnp.float32),
            pltpu.VMEM((4, BLOCK, SLAB), jnp.bfloat16),
            dma((NX, 4)), dma((NX, 4)), dma((NX,)), dma((NX,)),
            dma((4, 2)), dma((NZ,)), dma((3,)),
        ],
        compiler_params=pltpu.CompilerParams(
            collective_id=1, has_side_effects=True, vmem_limit_bytes=8 * 1024 * 1024),
        name="merge",
    )(partial, stats)


def per_device(queries, keys, values, block_mask, layout):
    kv, q, lists = gather(queries, keys, values, block_mask, layout)
    partial, stats = attend(lists, kv.reshape(KBLOCKS, BLOCK, 2 * SLAB), q.reshape(ITEMS, BLOCK, SLAB))
    return merge(partial, stats)


def solution(mesh):
    grid = Mesh(mesh.devices.reshape(NX, NY, 2, 4, 2), ("x", "y", "zh", "zl", "c"))
    rows = P(("x", "y", "zh", "zl", "c"), None)
    return jax.shard_map(
        per_device, mesh=grid,
        in_specs=(rows, rows, rows, P(("zl", "c"), None, None), P()),
        out_specs=rows, check_vma=False)
```

```python
import math

import jax
import jax.numpy as jnp
from jax import lax
from jax.experimental import pallas as pl
from jax.experimental.pallas import tpu as pltpu
from jax.sharding import Mesh, PartitionSpec as P

HEAD = 128
BLOCK = 128
HALF = 64
NX, NY, NZ = 4, 4, 8
HEADS_HERE = 3
SLAB = HEADS_HERE * HEAD
ITEMS = NX * (NZ // 2)
KBLOCKS = NY * NZ
LIST_ROWS = HEADS_HERE * ITEMS + 8
UNROLL = 4
WIDE = 2
NEG = -1e30
BIG = 1e30
COEF = math.log2(math.e) / math.sqrt(HEAD)
MESH = pl.DeviceIdType.MESH
ORDER = (1, 7, 2, 6, 3, 5, 4)


def place():
    x, y = lax.axis_index("x"), lax.axis_index("y")
    z = lax.axis_index("zh") * 4 + lax.axis_index("zl")
    return x, y, z, lax.axis_index("c")


def device(x, y, z, c):
    return (x, y, z // 4, z % 4, c)


def group(z):
    return (z % 4) * 2 + z // 4


def list_blocks(x, y, mask_in, layout_in, tables):
    shape = (BLOCK, BLOCK)
    down = lax.broadcasted_iota(jnp.int32, shape, 0)
    across = lax.broadcasted_iota(jnp.int32, shape, 1)

    def ones(hit):
        return jnp.where(hit, 1.0, 0.0).astype(jnp.bfloat16)

    def matmul(a, b):
        return jnp.dot(a, b, preferred_element_type=jnp.float32)

    held = ones(down == jnp.broadcast_to(layout_in[...], shape))
    stored_row = 32 * ((across >> 2) & 3) + 8 * y + 2 * (across & 3) + (across >> 4)
    rows = matmul(held, ones((down == stored_row) & (across < 2 * ITEMS))).T.astype(jnp.bfloat16)
    cols = matmul(held, ones((down == 32 * x + across) & (across < KBLOCKS))).astype(jnp.bfloat16)
    before = ones(down < across)
    lane = lax.broadcasted_iota(jnp.int32, (2 * ITEMS, BLOCK), 1)
    for head in range(HEADS_HERE):
        mask = mask_in[head].astype(jnp.float32).astype(jnp.bfloat16)
        some = matmul(rows, mask).astype(jnp.bfloat16)
        allowed = matmul(some, cols)
        rank = matmul(allowed.astype(jnp.bfloat16), before)[:2 * ITEMS]
        allowed = allowed[:2 * ITEMS]
        slot = jnp.where(allowed > 0.5, rank, -1.0)
        number = lane.astype(jnp.float32)
        table = jnp.where(lane == KBLOCKS, jnp.sum(allowed, axis=1, keepdims=True), 0.0)
        for p in range(KBLOCKS):
            found = jnp.sum(jnp.where(slot == float(p), number, 0.0), axis=1, keepdims=True)
            table = jnp.where(lane == p, found, table)
        table = table.astype(jnp.int32)
        for part in range(2):
            tables[part, head * ITEMS:(head + 1) * ITEMS] = table[part * ITEMS:(part + 1) * ITEMS]
    for part in range(2):
        tables[part, HEADS_HERE * ITEMS:] = jnp.zeros((8, BLOCK), jnp.int32)


def gather_kernel(q_in, k_in, v_in, mask_in, layout_in, kv, q, chosen,
                  zs_send, z_recv, q_send, q_recv, y_send, y_recv, f_send, f_recv,
                  s_send, s_recv, x_send, x_recv, xf_send, xf_recv, own, mask_sem, tables, mask_ref, layout_ref):
    x, y, z, c = place()
    other = 1 - c
    parity = z % 2
    yn, yp = (y + 1) % NY, (y + NY - 1) % NY
    xn, xp = (x + 1) % NX, (x + NX - 1) % NX
    y2, x2 = (y + 2) % NY, (x + 2) % NX

    def remote(src, dst, send, recv, dev):
        return pltpu.make_async_remote_copy(
            src_ref=src, dst_ref=dst, send_sem=send, recv_sem=recv,
            device_id=dev, device_id_type=MESH)

    mask_copy = pltpu.make_async_copy(mask_in, mask_ref, own.at[3])
    layout_copy = pltpu.make_async_copy(layout_in, layout_ref, own.at[4])
    mask_copy.start()
    layout_copy.start()
    barrier = pltpu.get_barrier_semaphore()
    peers = [device(x, y, (z + d) % NZ, cc) for d in range(1, NZ) for cc in range(2)]
    peers += [device(x, y, z, other), device(x, yn, z, c), device(x, yp, z, c),
              device(xn, y, z, c), device(xp, y, z, c)]
    for peer in peers:
        pl.semaphore_signal(barrier, inc=1, device_id=peer, device_id_type=MESH)
    pl.semaphore_wait(barrier, len(peers))

    def columns(zd):
        return pl.ds(pl.multiple_of(group(zd) * SLAB, SLAB), SLAB)

    def k_cols():
        return pl.ds(0, SLAB)

    def v_cols():
        return pl.ds(SLAB, SLAB)

    mine = columns(z)
    own_k = pltpu.make_async_copy(k_in.at[:, mine], kv.at[y, z, c, :, k_cols()], own.at[0])
    own_v = pltpu.make_async_copy(v_in.at[:, mine], kv.at[y, z, c, :, v_cols()], own.at[1])
    own_k.start()
    own_v.start()

    sends = []
    half = z // 2

    def start(copy):
        copy.start()
        sends.append(copy)

    def own_q_copies():
        return (
            pltpu.make_async_copy(q_in.at[:, mine], q.at[x, half, c], own.at[2]),
            remote(q_in.at[:, mine], q.at[x, half, c], q_send.at[0], q_recv.at[half, c],
                   device(x, y, z, other)),
        )

    for d in ORDER:
        zd = (z + d) % NZ
        cols = columns(zd)
        start(remote(k_in.at[:, cols], kv.at[y, z, c, :, k_cols()],
                     zs_send.at[0, d], z_recv.at[0, d], device(x, y, zd, c)))
        start(remote(v_in.at[:, cols], kv.at[y, z, c, :, v_cols()],
                     zs_send.at[1, d], z_recv.at[1, d], device(x, y, zd, c)))
        start(remote(q_in.at[:, cols], q.at[x, half, c],
                     q_send.at[d], q_recv.at[half, c], device(x, y, zd, parity)))

    @pl.when(c == parity)
    def _():
        own_q_copies()[0].start()

    @pl.when(c != parity)
    def _():
        own_q_copies()[1].start()

    mask_copy.wait()
    layout_copy.wait()
    list_blocks(x, y, mask_ref, layout_ref, tables)

    def waiter(dst, recv):
        return remote(dst, dst, recv, recv, device(x, y, z, other))

    def spread(d):
        zs = (z - d + NZ) % NZ
        piece = kv.at[y, zs, c]
        if d == 0:
            own_k.wait()
            own_v.wait()
        else:
            waiter(kv.at[y, zs, c, :, k_cols()], z_recv.at[0, d]).wait_recv()
            waiter(kv.at[y, zs, c, :, v_cols()], z_recv.at[1, d]).wait_recv()
        start(remote(piece, piece, y_send.at[0, d], y_recv.at[0, d], device(x, yn, z, c)))
        start(remote(piece, piece, y_send.at[1, d], y_recv.at[1, d], device(x, yp, z, c)))
        start(remote(piece, piece, s_send.at[0, d], s_recv.at[0, d], device(x, y, z, other)))

    def relay(d):
        zs = (z - d + NZ) % NZ
        for way, (row, ahead) in enumerate(((yp, yn), (yn, yp))):
            piece = kv.at[row, zs, c]
            waiter(piece, y_recv.at[way, d]).wait_recv()
            if d % 2 == way:
                start(remote(piece, piece, f_send.at[d], f_recv.at[d], device(x, ahead, z, c)))
            start(remote(piece, piece, s_send.at[1 + way, d], s_recv.at[1 + way, d],
                         device(x, y, z, other)))

    odd = (z + c) % 2
    q_order = []
    for even_d, odd_d in zip((0, 2, 6, 4), (1, 7, 3, 5)):
        q_order.append(((z - even_d - odd * (odd_d - even_d) + NZ) % NZ) // 2)

    def spread_q(k):
        i = q_order[k]
        for cc in range(2):
            piece = q.at[x, i, cc]
            local = (c == parity) & (i == half) & (c == cc)

            @pl.when(local)
            def _():
                own_q_copies()[0].wait()

            @pl.when(jnp.logical_not(local))
            def _():
                waiter(piece, q_recv.at[i, cc]).wait_recv()

        piece = q.at[x, i]
        start(remote(piece, piece, x_send.at[0, k], x_recv.at[0, k], device(xn, y, z, c)))
        start(remote(piece, piece, x_send.at[1, k], x_recv.at[1, k], device(xp, y, z, c)))

    def relay_q(k):
        for way, (row, ahead) in enumerate(((xp, xn), (xn, xp))):
            piece = q.at[row, q_order[k]]
            waiter(piece, x_recv.at[way, k]).wait_recv()
            if k % 2 == way:
                start(remote(piece, piece, xf_send.at[k], xf_recv.at[k], device(ahead, y, z, c)))

    seq = (0,) + ORDER
    for step in range(len(seq) + 2):
        if step < len(seq):
            spread(seq[step])
        if step >= 2:
            relay(seq[step - 2])
        if step % 2 and step < len(seq):
            spread_q(step // 2)
        if step in (4, 6, 8, 9):
            relay_q((4, 6, 8, 9).index(step))
    for d in seq:
        zs = (z - d + NZ) % NZ
        piece = kv.at[y2, zs, c]
        waiter(piece, f_recv.at[d]).wait_recv()
        start(remote(piece, piece, s_send.at[3, d], s_recv.at[3, d], device(x, y, z, other)))
    for k in range(4):
        waiter(q.at[x2, q_order[k]], xf_recv.at[k]).wait_recv()
    def give():
        return remote(tables.at[other], chosen, mask_sem.at[0], mask_sem.at[1], device(x, y, z, other))

    def keep():
        return pltpu.make_async_copy(tables.at[c], chosen, mask_sem.at[2])

    @pl.when(c == z // 4)
    def _():
        give().start()
        keep().start()

    for d in seq:
        zs = (z - d + NZ) % NZ
        for slot, row in enumerate((y, yp, yn, y2)):
            waiter(kv.at[row, zs, other], s_recv.at[slot, d]).wait_recv()

    @pl.when(c == z // 4)
    def _():
        give().wait_send()
        keep().wait()

    @pl.when(c != z // 4)
    def _():
        give().wait_recv()


    @pl.when(c != parity)
    def _():
        own_q_copies()[1].wait_send()

    for copy in sends:
        copy.wait_send()


def gather(queries, keys, values, block_mask, layout):
    any_space = pl.BlockSpec(memory_space=pl.ANY)
    hbm = pl.BlockSpec(memory_space=pltpu.HBM)
    dma = pltpu.SemaphoreType.DMA
    return pl.pallas_call(
        gather_kernel,
        out_shape=(
            jax.ShapeDtypeStruct((NY, NZ, 2, HALF, 2 * SLAB), jnp.bfloat16),
            jax.ShapeDtypeStruct((NX, NZ // 2, 2, HALF, SLAB), jnp.bfloat16),
            jax.ShapeDtypeStruct((LIST_ROWS, BLOCK), jnp.int32),
        ),
        in_specs=[hbm] * 5,
        out_specs=(any_space, any_space, any_space),
        scratch_shapes=[
            dma((2, NZ)), dma((2, NZ)), dma((NZ,)), dma((4, 2)),
            dma((2, NZ)), dma((2, NZ)), dma((NZ,)), dma((NZ,)),
            dma((4, NZ)), dma((4, NZ)),
            dma((2, 4)), dma((2, 4)), dma((4,)), dma((4,)), dma((5,)), dma((3,)),
            pltpu.VMEM((2, LIST_ROWS, BLOCK), jnp.int32),
            pltpu.VMEM((HEADS_HERE, BLOCK, BLOCK), jnp.int32),
            pltpu.VMEM((1, BLOCK), jnp.int32),
        ],
        compiler_params=pltpu.CompilerParams(
            collective_id=0, has_side_effects=True, vmem_limit_bytes=8 * 1024 * 1024),
        name="gather",
    )(*(pltpu.with_memory_space_constraint(a, pltpu.HBM)
        for a in (queries, keys, values, block_mask, layout.reshape(1, -1))))


def attend_kernel(lists, kv_ref, q_ref, o_ref, stat_ref, vt, qt, s_ref, p_ref, acc, m_ref, l_ref):
    total_items = HEADS_HERE * ITEMS

    def block(item, column):
        return lists[item, column]

    def count_of(item):
        return block(item, KBLOCKS)

    acc[...] = jnp.zeros_like(acc)
    m_ref[...] = jnp.full_like(m_ref, NEG)
    l_ref[...] = jnp.zeros_like(l_ref)
    s_ref[...] = jnp.zeros_like(s_ref)
    p_ref[...] = jnp.zeros_like(p_ref)
    qt[total_items] = jnp.zeros((HEAD, BLOCK), jnp.bfloat16)

    for head in range(HEADS_HERE):
        @pl.loop(0, KBLOCKS, step=4)
        def _(b, head=head):
            for u in range(4):
                vt[head * KBLOCKS + b + u] = kv_ref[b + u, :, SLAB + head * HEAD:SLAB + (head + 1) * HEAD].T

        @pl.loop(0, ITEMS, step=4)
        def _(i, head=head):
            for u in range(4):
                qt[head * ITEMS + i + u] = q_ref[i + u, :, head * HEAD:(head + 1) * HEAD].T

    def steps_of(item):
        return jnp.maximum((count_of(item) + UNROLL - 1) >> 2, 1)

    steps = lax.fori_loop(0, total_items, lambda i, n: n + steps_of(i), 0)

    def home(item):
        spare = item == total_items
        return jnp.where(spare, ITEMS, item & (ITEMS - 1)), jnp.where(spare, 0, item >> 4)

    def score(item, at, out):
        left = count_of(item) - at
        cols = pl.ds(pl.multiple_of(home(item)[1] * HEAD, HEAD), HEAD)
        rows = [kv_ref[block(item, at + u), :, cols] for u in range(UNROLL)]
        t = jnp.dot(jnp.concatenate(rows, axis=0), qt[item], preferred_element_type=jnp.float32) * COEF
        out[...] = t
        peak = jnp.full((1, BLOCK), NEG, jnp.float32)
        for u in range(UNROLL):
            part = jnp.max(t[u * BLOCK:(u + 1) * BLOCK], axis=0, keepdims=True)
            peak = jnp.maximum(peak, jnp.where(u < left, part, NEG))
        return peak

    def soften(chunk, peak, src, out):
        item, at = chunk
        first = at == 0
        left = count_of(item) - at
        m_old = jnp.where(first, NEG, m_ref[...])
        m_new = jnp.maximum(m_old, peak)
        alpha = jnp.where(first, 0.0, jnp.exp2(m_old - m_new))
        summed = l_ref[...] * alpha
        for u in range(UNROLL):
            rows = slice(u * BLOCK, (u + 1) * BLOCK)
            p = jnp.exp2(src[rows] - jnp.where(u < left, m_new, BIG))
            summed = summed + jnp.sum(p, axis=0, keepdims=True)
            out[rows] = p.astype(jnp.bfloat16)
        m_ref[...] = m_new
        l_ref[...] = summed

        where, head = home(item)
        stat_ref[where, pl.ds(2 * head, 1), :] = m_new
        stat_ref[where, pl.ds(2 * head + 1, 1), :] = summed
        return alpha

    def gather_values(chunk, alpha, src):
        item, at = chunk
        where, head = home(item)
        cols = [vt[head * KBLOCKS + block(item, at + u)] for u in range(UNROLL)]
        value = acc[...] * alpha + jnp.dot(jnp.concatenate(cols, axis=1), src[...],
                                           preferred_element_type=jnp.float32)
        acc[...] = value
        o_ref[where, pl.ds(pl.multiple_of(head * HEAD, HEAD), HEAD), :] = value.astype(jnp.bfloat16)

    def advance(chunk):
        item, at = chunk
        done = at + UNROLL >= count_of(item)
        return jnp.minimum(jnp.where(done, item + 1, item), total_items), jnp.where(done, 0, at + UNROLL)

    start = (jnp.int32(0), jnp.int32(0))
    spare = (jnp.int32(total_items), jnp.int32(0))

    def group_step(_, state):
        at, chunks_b, chunks_c, peaks, alphas = state
        chunks_a = []
        for _ in range(WIDE):
            chunks_a.append(at)
            at = advance(at)
        for w in range(WIDE):
            gather_values(chunks_c[w], alphas[w], p_ref.at[w])
        alphas = [soften(chunks_b[w], peaks[w], s_ref.at[w], p_ref.at[w]) for w in range(WIDE)]
        peaks = [score(*chunks_a[w], s_ref.at[w]) for w in range(WIDE)]
        return at, tuple(chunks_a), chunks_b, tuple(peaks), tuple(alphas)

    lax.fori_loop(0, (steps + WIDE - 1) // WIDE + 2, group_step, (
        start, (spare,) * WIDE, (spare,) * WIDE,
        (jnp.full((1, BLOCK), NEG, jnp.float32),) * WIDE, (jnp.zeros((1, BLOCK), jnp.float32),) * WIDE))


def attend(lists, kv, queries):
    vmem = pl.BlockSpec(memory_space=pltpu.VMEM)
    smem = pl.BlockSpec(memory_space=pltpu.SMEM)
    return pl.pallas_call(
        attend_kernel,
        out_shape=(
            jax.ShapeDtypeStruct((ITEMS + 1, SLAB, BLOCK), jnp.bfloat16),
            jax.ShapeDtypeStruct((ITEMS + 1, 8, BLOCK), jnp.float32),
        ),
        in_specs=[smem, vmem, vmem],
        out_specs=(vmem, vmem),
        scratch_shapes=[
            pltpu.VMEM((HEADS_HERE * KBLOCKS, HEAD, BLOCK), jnp.bfloat16),
            pltpu.VMEM((HEADS_HERE * ITEMS + 1, HEAD, BLOCK), jnp.bfloat16),
            pltpu.VMEM((WIDE, UNROLL * BLOCK, BLOCK), jnp.float32),
            pltpu.VMEM((WIDE, UNROLL * BLOCK, BLOCK), jnp.bfloat16),
            pltpu.VMEM((HEAD, BLOCK), jnp.float32),
            pltpu.VMEM((1, BLOCK), jnp.float32),
            pltpu.VMEM((1, BLOCK), jnp.float32),
        ],
        compiler_params=pltpu.CompilerParams(vmem_limit_bytes=24 * 1024 * 1024),
        name="attend",
    )(lists, kv, queries)


def merge_kernel(o_in, stat_in, out, o_all, stat_all, result, x_send, x_recv, st_send, st_recv,
                 z_send, z_recv, own):
    x, y, z, c = place()
    other = 1 - c

    def remote(src, dst, send, recv, dev):
        return pltpu.make_async_remote_copy(
            src_ref=src, dst_ref=dst, send_sem=send, recv_sem=recv,
            device_id=dev, device_id_type=MESH)

    barrier = pltpu.get_barrier_semaphore()
    peers = [device(x, y, (z + d) % NZ, cc) for d in range(1, NZ) for cc in range(2)]
    peers += [device(x, y, z, other)] + [device((x + d) % NX, y, z, c) for d in range(1, NX)]
    for peer in peers:
        pl.semaphore_signal(barrier, inc=1, device_id=peer, device_id_type=MESH)
    pl.semaphore_wait(barrier, len(peers))

    shift = (2, 1, 3, 0)
    rows_of = [(z // 2 + r) % 4 for r in shift]
    sends = []
    for k in range(4):
        for d in (2, 1, 3):
            xd = (x + d) % NX
            dev = device(xd, y, z, c)
            if k == 0:
                sends.append(remote(stat_in.at[pl.ds(4 * xd, 4)], stat_all.at[x], st_send.at[d], st_recv.at[d], dev))
                sends[-1].start()
            sends.append(remote(o_in.at[4 * xd + rows_of[k]], o_all.at[x, k], x_send.at[d, k], x_recv.at[d, k], dev))
            sends[-1].start()
    keep = [pltpu.make_async_copy(o_in.at[4 * x + rows_of[k]], o_all.at[x, k], own.at[k]) for k in range(4)]
    keep.append(pltpu.make_async_copy(stat_in.at[pl.ds(4 * x, 4)], stat_all.at[x], own.at[4]))
    for copy in keep:
        copy.start()

    def waiter(dst, recv):
        return remote(dst, dst, recv, recv, device(x, y, z, other))

    for copy in keep:
        copy.wait()
    for d in (1, 3, 2):
        waiter(stat_all.at[(x - d + NX) % NX], st_recv.at[d]).wait_recv()

    def columns(zd):
        return pl.ds(pl.multiple_of(group(zd) * SLAB, SLAB), SLAB)

    def local_of(k, cc):
        src = result.at[k, pl.ds(cc * HALF, HALF)]
        return pltpu.make_async_copy(src, out.at[:, columns(z)], own.at[5])

    def remote_of(k, cc):
        src = result.at[k, pl.ds(cc * HALF, HALF)]
        return remote(src, out.at[:, columns(z)], z_send.at[k, cc], z_recv.at[z],
                      device(x, y, 2 * rows_of[k] + c, cc))

    def deliver(k, act_local, act_remote):
        for cc in range(2):
            if shift[k]:
                act_remote(remote_of(k, cc))
                continue
            here = (z % 2 == c) & (c == cc)

            @pl.when(here)
            def _(cc=cc):
                act_local(local_of(k, cc))

            @pl.when(jnp.logical_not(here))
            def _(cc=cc):
                act_remote(remote_of(k, cc))

    def ship(k):
        deliver(k, lambda copy: copy.start(), lambda copy: copy.start())

    for k in range(4):
        for d in (1, 3, 2):
            waiter(o_all.at[(x - d + NX) % NX, k], x_recv.at[d, k]).wait_recv()
        for head in range(HEADS_HERE):
            m = [stat_all[s, rows_of[k], 2 * head:2 * head + 1, :] for s in range(NX)]
            top = jnp.maximum(jnp.maximum(m[0], m[1]), jnp.maximum(m[2], m[3]))
            w = [jnp.exp2(v - top) for v in m]
            total = sum(w[s] * stat_all[s, rows_of[k], 2 * head + 1:2 * head + 2, :] for s in range(NX))
            rows = slice(head * HEAD, (head + 1) * HEAD)
            share = 1.0 / total
            value = sum(o_all[s, k, rows, :].astype(jnp.float32) * (w[s] * share) for s in range(NX))
            result[k, :, rows] = value.T.astype(jnp.bfloat16)
        if k:
            ship(k - 1)
    ship(3)

    for zs in range(NZ):
        local = (zs == z) & (zs % 2 == c)

        @pl.when(jnp.logical_not(local))
        def _(zs=zs):
            waiter(out.at[:, columns(zs)], z_recv.at[zs]).wait_recv()
    for k in range(4):
        deliver(k, lambda copy: copy.wait(), lambda copy: copy.wait_send())
    for copy in sends:
        copy.wait_send()


def merge(partial, stats):
    any_space = pl.BlockSpec(memory_space=pl.ANY)
    dma = pltpu.SemaphoreType.DMA
    return pl.pallas_call(
        merge_kernel,
        out_shape=jax.ShapeDtypeStruct((HALF, NZ * SLAB), jnp.bfloat16),
        in_specs=[any_space, any_space],
        out_specs=any_space,
        scratch_shapes=[
            pltpu.VMEM((NX, 4, SLAB, BLOCK), jnp.bfloat16),
            pltpu.VMEM((NX, 4, 8, BLOCK), jnp.float32),
            pltpu.VMEM((4, BLOCK, SLAB), jnp.bfloat16),
            dma((NX, 4)), dma((NX, 4)), dma((NX,)), dma((NX,)),
            dma((4, 2)), dma((NZ,)), dma((6,)),
        ],
        compiler_params=pltpu.CompilerParams(
            collective_id=1, has_side_effects=True, vmem_limit_bytes=8 * 1024 * 1024),
        name="merge",
    )(partial, stats)


def per_device(queries, keys, values, block_mask, layout):
    kv, q, lists = gather(queries, keys, values, block_mask, layout)
    partial, stats = attend(lists, kv.reshape(KBLOCKS, BLOCK, 2 * SLAB), q.reshape(ITEMS, BLOCK, SLAB))
    return merge(partial, stats)


def solution(mesh):
    grid = Mesh(mesh.devices.reshape(NX, NY, 2, 4, 2), ("x", "y", "zh", "zl", "c"))
    rows = P(("x", "y", "zh", "zl", "c"), None)
    return jax.shard_map(
        per_device, mesh=grid,
        in_specs=(rows, rows, rows, P(("zl", "c"), None, None), P()),
        out_specs=rows, check_vma=False)
```

```python
import math

import jax
import jax.numpy as jnp
from jax import lax
from jax.experimental import pallas as pl
from jax.experimental.pallas import tpu as pltpu
from jax.sharding import Mesh, PartitionSpec as P

HEAD = 128
BLOCK = 128
HALF = 64
NX, NY, NZ = 4, 4, 8
HEADS_HERE = 3
SLAB = HEADS_HERE * HEAD
ITEMS = NX * (NZ // 2)
KBLOCKS = NY * NZ
LIST_ROWS = HEADS_HERE * ITEMS + 8
UNROLL = 4
WIDE = 6
NEG = -1e30
BIG = 1e30
COEF = math.log2(math.e) / math.sqrt(HEAD)
MESH = pl.DeviceIdType.MESH
ORDER = (1, 7, 2, 6, 3, 5, 4)


def place():
    x, y = lax.axis_index("x"), lax.axis_index("y")
    z = lax.axis_index("zh") * 4 + lax.axis_index("zl")
    return x, y, z, lax.axis_index("c")


def device(x, y, z, c):
    return (x, y, z // 4, z % 4, c)


def group(z):
    return (z % 4) * 2 + z // 4


def list_blocks(x, y, mask_in, layout_in, tables):
    shape = (BLOCK, BLOCK)
    down = lax.broadcasted_iota(jnp.int32, shape, 0)
    across = lax.broadcasted_iota(jnp.int32, shape, 1)

    def ones(hit):
        return jnp.where(hit, 1.0, 0.0).astype(jnp.bfloat16)

    def matmul(a, b):
        return jnp.dot(a, b, preferred_element_type=jnp.float32)

    held = ones(down == jnp.broadcast_to(layout_in[...], shape))
    stored_row = 32 * ((across >> 2) & 3) + 8 * y + 2 * (across & 3) + (across >> 4)
    rows = matmul(held, ones((down == stored_row) & (across < 2 * ITEMS))).T.astype(jnp.bfloat16)
    cols = matmul(held, ones((down == 32 * x + across) & (across < KBLOCKS))).astype(jnp.bfloat16)
    before = ones(down < across)
    lane = lax.broadcasted_iota(jnp.int32, (2 * ITEMS, BLOCK), 1)
    for head in range(HEADS_HERE):
        mask = mask_in[head].astype(jnp.float32).astype(jnp.bfloat16)
        some = matmul(rows, mask).astype(jnp.bfloat16)
        allowed = matmul(some, cols)
        rank = matmul(allowed.astype(jnp.bfloat16), before)[:2 * ITEMS]
        allowed = allowed[:2 * ITEMS]
        slot = jnp.where(allowed > 0.5, rank, -1.0)
        number = lane.astype(jnp.float32)
        table = jnp.where(lane == KBLOCKS, jnp.sum(allowed, axis=1, keepdims=True), 0.0)
        for p in range(KBLOCKS):
            found = jnp.sum(jnp.where(slot == float(p), number, 0.0), axis=1, keepdims=True)
            table = jnp.where(lane == p, found, table)
        table = table.astype(jnp.int32)
        for part in range(2):
            tables[part, head * ITEMS:(head + 1) * ITEMS] = table[part * ITEMS:(part + 1) * ITEMS]
    for part in range(2):
        tables[part, HEADS_HERE * ITEMS:] = jnp.zeros((8, BLOCK), jnp.int32)


def gather_kernel(q_in, k_in, v_in, mask_in, layout_in, kv, q, chosen,
                  zs_send, z_recv, q_send, q_recv, y_send, y_recv, f_send, f_recv,
                  s_send, s_recv, x_send, x_recv, xf_send, xf_recv, own, mask_sem, tables, mask_ref, layout_ref):
    x, y, z, c = place()
    other = 1 - c
    parity = z % 2
    yn, yp = (y + 1) % NY, (y + NY - 1) % NY
    xn, xp = (x + 1) % NX, (x + NX - 1) % NX
    y2, x2 = (y + 2) % NY, (x + 2) % NX

    def remote(src, dst, send, recv, dev):
        return pltpu.make_async_remote_copy(
            src_ref=src, dst_ref=dst, send_sem=send, recv_sem=recv,
            device_id=dev, device_id_type=MESH)

    mask_copy = pltpu.make_async_copy(mask_in, mask_ref, own.at[3])
    layout_copy = pltpu.make_async_copy(layout_in, layout_ref, own.at[4])
    mask_copy.start()
    layout_copy.start()
    barrier = pltpu.get_barrier_semaphore()
    peers = [device(x, y, (z + d) % NZ, cc) for d in range(1, NZ) for cc in range(2)]
    peers += [device(x, y, z, other), device(x, yn, z, c), device(x, yp, z, c),
              device(xn, y, z, c), device(xp, y, z, c)]
    for peer in peers:
        pl.semaphore_signal(barrier, inc=1, device_id=peer, device_id_type=MESH)
    pl.semaphore_wait(barrier, len(peers))

    def columns(zd):
        return pl.ds(pl.multiple_of(group(zd) * SLAB, SLAB), SLAB)

    def k_cols():
        return pl.ds(0, SLAB)

    def v_cols():
        return pl.ds(SLAB, SLAB)

    mine = columns(z)
    own_k = pltpu.make_async_copy(k_in.at[:, mine], kv.at[y, z, c, :, k_cols()], own.at[0])
    own_v = pltpu.make_async_copy(v_in.at[:, mine], kv.at[y, z, c, :, v_cols()], own.at[1])
    own_k.start()
    own_v.start()

    sends = []
    half = z // 2

    def start(copy):
        copy.start()
        sends.append(copy)

    def own_q_copies():
        return (
            pltpu.make_async_copy(q_in.at[:, mine], q.at[x, half, c], own.at[2]),
            remote(q_in.at[:, mine], q.at[x, half, c], q_send.at[0], q_recv.at[half, c],
                   device(x, y, z, other)),
        )

    for d in ORDER:
        zd = (z + d) % NZ
        cols = columns(zd)
        start(remote(k_in.at[:, cols], kv.at[y, z, c, :, k_cols()],
                     zs_send.at[0, d], z_recv.at[0, d], device(x, y, zd, c)))
        start(remote(v_in.at[:, cols], kv.at[y, z, c, :, v_cols()],
                     zs_send.at[1, d], z_recv.at[1, d], device(x, y, zd, c)))
        start(remote(q_in.at[:, cols], q.at[x, half, c],
                     q_send.at[d], q_recv.at[half, c], device(x, y, zd, parity)))

    @pl.when(c == parity)
    def _():
        own_q_copies()[0].start()

    @pl.when(c != parity)
    def _():
        own_q_copies()[1].start()

    mask_copy.wait()
    layout_copy.wait()
    list_blocks(x, y, mask_ref, layout_ref, tables)

    def waiter(dst, recv):
        return remote(dst, dst, recv, recv, device(x, y, z, other))

    def spread(d):
        zs = (z - d + NZ) % NZ
        piece = kv.at[y, zs, c]
        if d == 0:
            own_k.wait()
            own_v.wait()
        else:
            waiter(kv.at[y, zs, c, :, k_cols()], z_recv.at[0, d]).wait_recv()
            waiter(kv.at[y, zs, c, :, v_cols()], z_recv.at[1, d]).wait_recv()
        start(remote(piece, piece, y_send.at[0, d], y_recv.at[0, d], device(x, yn, z, c)))
        start(remote(piece, piece, y_send.at[1, d], y_recv.at[1, d], device(x, yp, z, c)))
        start(remote(piece, piece, s_send.at[0, d], s_recv.at[0, d], device(x, y, z, other)))

    def relay(d):
        zs = (z - d + NZ) % NZ
        for way, (row, ahead) in enumerate(((yp, yn), (yn, yp))):
            piece = kv.at[row, zs, c]
            waiter(piece, y_recv.at[way, d]).wait_recv()
            if d % 2 == way:
                start(remote(piece, piece, f_send.at[d], f_recv.at[d], device(x, ahead, z, c)))
            start(remote(piece, piece, s_send.at[1 + way, d], s_recv.at[1 + way, d],
                         device(x, y, z, other)))

    odd = (z + c) % 2
    q_order = []
    for even_d, odd_d in zip((0, 2, 6, 4), (1, 7, 3, 5)):
        q_order.append(((z - even_d - odd * (odd_d - even_d) + NZ) % NZ) // 2)

    def spread_q(k):
        i = q_order[k]
        for cc in range(2):
            piece = q.at[x, i, cc]
            local = (c == parity) & (i == half) & (c == cc)

            @pl.when(local)
            def _():
                own_q_copies()[0].wait()

            @pl.when(jnp.logical_not(local))
            def _():
                waiter(piece, q_recv.at[i, cc]).wait_recv()

        piece = q.at[x, i]
        start(remote(piece, piece, x_send.at[0, k], x_recv.at[0, k], device(xn, y, z, c)))
        start(remote(piece, piece, x_send.at[1, k], x_recv.at[1, k], device(xp, y, z, c)))

    def relay_q(k):
        for way, (row, ahead) in enumerate(((xp, xn), (xn, xp))):
            piece = q.at[row, q_order[k]]
            waiter(piece, x_recv.at[way, k]).wait_recv()
            if k % 2 == way:
                start(remote(piece, piece, xf_send.at[k], xf_recv.at[k], device(ahead, y, z, c)))

    seq = (0,) + ORDER
    for step in range(len(seq) + 2):
        if step < len(seq):
            spread(seq[step])
        if step >= 2:
            relay(seq[step - 2])
        if step % 2 and step < len(seq):
            spread_q(step // 2)
        if step in (4, 6, 8, 9):
            relay_q((4, 6, 8, 9).index(step))
    for d in seq:
        zs = (z - d + NZ) % NZ
        piece = kv.at[y2, zs, c]
        waiter(piece, f_recv.at[d]).wait_recv()
        start(remote(piece, piece, s_send.at[3, d], s_recv.at[3, d], device(x, y, z, other)))
    for k in range(4):
        waiter(q.at[x2, q_order[k]], xf_recv.at[k]).wait_recv()
    def give():
        return remote(tables.at[other], chosen, mask_sem.at[0], mask_sem.at[1], device(x, y, z, other))

    def keep():
        return pltpu.make_async_copy(tables.at[c], chosen, mask_sem.at[2])

    @pl.when(c == z // 4)
    def _():
        give().start()
        keep().start()

    for d in seq:
        zs = (z - d + NZ) % NZ
        for slot, row in enumerate((y, yp, yn, y2)):
            waiter(kv.at[row, zs, other], s_recv.at[slot, d]).wait_recv()

    @pl.when(c == z // 4)
    def _():
        give().wait_send()
        keep().wait()

    @pl.when(c != z // 4)
    def _():
        give().wait_recv()


    @pl.when(c != parity)
    def _():
        own_q_copies()[1].wait_send()

    for copy in sends:
        copy.wait_send()


def gather(queries, keys, values, block_mask, layout):
    any_space = pl.BlockSpec(memory_space=pl.ANY)
    hbm = pl.BlockSpec(memory_space=pltpu.HBM)
    dma = pltpu.SemaphoreType.DMA
    return pl.pallas_call(
        gather_kernel,
        out_shape=(
            jax.ShapeDtypeStruct((NY, NZ, 2, HALF, 2 * SLAB), jnp.bfloat16),
            jax.ShapeDtypeStruct((NX, NZ // 2, 2, HALF, SLAB), jnp.bfloat16),
            jax.ShapeDtypeStruct((LIST_ROWS, BLOCK), jnp.int32),
        ),
        in_specs=[hbm] * 5,
        out_specs=(any_space, any_space, any_space),
        scratch_shapes=[
            dma((2, NZ)), dma((2, NZ)), dma((NZ,)), dma((4, 2)),
            dma((2, NZ)), dma((2, NZ)), dma((NZ,)), dma((NZ,)),
            dma((4, NZ)), dma((4, NZ)),
            dma((2, 4)), dma((2, 4)), dma((4,)), dma((4,)), dma((5,)), dma((3,)),
            pltpu.VMEM((2, LIST_ROWS, BLOCK), jnp.int32),
            pltpu.VMEM((HEADS_HERE, BLOCK, BLOCK), jnp.int32),
            pltpu.VMEM((1, BLOCK), jnp.int32),
        ],
        compiler_params=pltpu.CompilerParams(
            collective_id=0, has_side_effects=True, vmem_limit_bytes=8 * 1024 * 1024),
        name="gather",
    )(*(pltpu.with_memory_space_constraint(a, pltpu.HBM)
        for a in (queries, keys, values, block_mask, layout.reshape(1, -1))))


def attend_kernel(lists, kv_ref, q_ref, o_ref, stat_ref, vt, qt, s_ref, p_ref, acc, m_ref, l_ref):
    total_items = HEADS_HERE * ITEMS

    def block(item, column):
        return lists[item, column]

    def count_of(item):
        return block(item, KBLOCKS)

    acc[...] = jnp.zeros_like(acc)
    m_ref[...] = jnp.full_like(m_ref, NEG)
    l_ref[...] = jnp.zeros_like(l_ref)
    s_ref[...] = jnp.zeros_like(s_ref)
    p_ref[...] = jnp.zeros_like(p_ref)
    qt[total_items] = jnp.zeros((HEAD, BLOCK), jnp.bfloat16)

    for head in range(HEADS_HERE):
        @pl.loop(0, KBLOCKS, step=4)
        def _(b, head=head):
            for u in range(4):
                vt[head * KBLOCKS + b + u] = kv_ref[b + u, :, SLAB + head * HEAD:SLAB + (head + 1) * HEAD].T

        @pl.loop(0, ITEMS, step=4)
        def _(i, head=head):
            for u in range(4):
                qt[head * ITEMS + i + u] = q_ref[i + u, :, head * HEAD:(head + 1) * HEAD].T

    def steps_of(item):
        return jnp.maximum((count_of(item) + UNROLL - 1) >> 2, 1)

    steps = lax.fori_loop(0, total_items, lambda i, n: n + steps_of(i), 0)

    def home(item):
        spare = item == total_items
        return jnp.where(spare, ITEMS, item & (ITEMS - 1)), jnp.where(spare, 0, item >> 4)

    def score(item, at, out):
        left = count_of(item) - at
        cols = pl.ds(pl.multiple_of(home(item)[1] * HEAD, HEAD), HEAD)
        rows = [kv_ref[block(item, at + u), :, cols] for u in range(UNROLL)]
        t = jnp.dot(jnp.concatenate(rows, axis=0), qt[item], preferred_element_type=jnp.float32) * COEF
        out[...] = t
        peak = jnp.full((1, BLOCK), NEG, jnp.float32)
        for u in range(UNROLL):
            part = jnp.max(t[u * BLOCK:(u + 1) * BLOCK], axis=0, keepdims=True)
            peak = jnp.maximum(peak, jnp.where(u < left, part, NEG))
        return peak

    def soften(chunk, peak, src, out):
        item, at = chunk
        first = at == 0
        left = count_of(item) - at
        m_old = jnp.where(first, NEG, m_ref[...])
        m_new = jnp.maximum(m_old, peak)
        alpha = jnp.where(first, 0.0, jnp.exp2(m_old - m_new))
        summed = l_ref[...] * alpha
        for u in range(UNROLL):
            rows = slice(u * BLOCK, (u + 1) * BLOCK)
            p = jnp.exp2(src[rows] - jnp.where(u < left, m_new, BIG))
            summed = summed + jnp.sum(p, axis=0, keepdims=True)
            out[rows] = p.astype(jnp.bfloat16)
        m_ref[...] = m_new
        l_ref[...] = summed

        where, head = home(item)
        stat_ref[where, pl.ds(2 * head, 1), :] = m_new
        stat_ref[where, pl.ds(2 * head + 1, 1), :] = summed
        return alpha

    def gather_values(chunk, alpha, src):
        item, at = chunk
        where, head = home(item)
        cols = [vt[head * KBLOCKS + block(item, at + u)] for u in range(UNROLL)]
        value = acc[...] * alpha + jnp.dot(jnp.concatenate(cols, axis=1), src[...],
                                           preferred_element_type=jnp.float32)
        acc[...] = value
        o_ref[where, pl.ds(pl.multiple_of(head * HEAD, HEAD), HEAD), :] = value.astype(jnp.bfloat16)

    def advance(chunk):
        item, at = chunk
        done = at + UNROLL >= count_of(item)
        return jnp.minimum(jnp.where(done, item + 1, item), total_items), jnp.where(done, 0, at + UNROLL)

    start = (jnp.int32(0), jnp.int32(0))
    spare = (jnp.int32(total_items), jnp.int32(0))

    def group_step(_, state):
        at, chunks_b, chunks_c, peaks, alphas = state
        chunks_a = []
        for _ in range(WIDE):
            chunks_a.append(at)
            at = advance(at)
        for w in range(WIDE):
            gather_values(chunks_c[w], alphas[w], p_ref.at[w])
        alphas = [soften(chunks_b[w], peaks[w], s_ref.at[w], p_ref.at[w]) for w in range(WIDE)]
        peaks = [score(*chunks_a[w], s_ref.at[w]) for w in range(WIDE)]
        return at, tuple(chunks_a), chunks_b, tuple(peaks), tuple(alphas)

    lax.fori_loop(0, (steps + WIDE - 1) // WIDE + 2, group_step, (
        start, (spare,) * WIDE, (spare,) * WIDE,
        (jnp.full((1, BLOCK), NEG, jnp.float32),) * WIDE, (jnp.zeros((1, BLOCK), jnp.float32),) * WIDE))


def attend(lists, kv, queries):
    vmem = pl.BlockSpec(memory_space=pltpu.VMEM)
    smem = pl.BlockSpec(memory_space=pltpu.SMEM)
    return pl.pallas_call(
        attend_kernel,
        out_shape=(
            jax.ShapeDtypeStruct((ITEMS + 1, SLAB, BLOCK), jnp.bfloat16),
            jax.ShapeDtypeStruct((ITEMS + 1, 8, BLOCK), jnp.float32),
        ),
        in_specs=[smem, vmem, vmem],
        out_specs=(vmem, vmem),
        scratch_shapes=[
            pltpu.VMEM((HEADS_HERE * KBLOCKS, HEAD, BLOCK), jnp.bfloat16),
            pltpu.VMEM((HEADS_HERE * ITEMS + 1, HEAD, BLOCK), jnp.bfloat16),
            pltpu.VMEM((WIDE, UNROLL * BLOCK, BLOCK), jnp.float32),
            pltpu.VMEM((WIDE, UNROLL * BLOCK, BLOCK), jnp.bfloat16),
            pltpu.VMEM((HEAD, BLOCK), jnp.float32),
            pltpu.VMEM((1, BLOCK), jnp.float32),
            pltpu.VMEM((1, BLOCK), jnp.float32),
        ],
        compiler_params=pltpu.CompilerParams(vmem_limit_bytes=24 * 1024 * 1024),
        name="attend",
    )(lists, kv, queries)


def merge_kernel(o_in, stat_in, out, o_all, stat_all, result, x_send, x_recv, st_send, st_recv,
                 z_send, z_recv, own):
    x, y, z, c = place()
    other = 1 - c

    def remote(src, dst, send, recv, dev):
        return pltpu.make_async_remote_copy(
            src_ref=src, dst_ref=dst, send_sem=send, recv_sem=recv,
            device_id=dev, device_id_type=MESH)

    barrier = pltpu.get_barrier_semaphore()
    peers = [device(x, y, (z + d) % NZ, cc) for d in range(1, NZ) for cc in range(2)]
    peers += [device(x, y, z, other)] + [device((x + d) % NX, y, z, c) for d in range(1, NX)]
    for peer in peers:
        pl.semaphore_signal(barrier, inc=1, device_id=peer, device_id_type=MESH)
    pl.semaphore_wait(barrier, len(peers))

    shift = (2, 1, 3, 0)
    rows_of = [(z // 2 + r) % 4 for r in shift]
    sends = []
    for k in range(4):
        for d in (2, 1, 3):
            xd = (x + d) % NX
            dev = device(xd, y, z, c)
            if k == 0:
                sends.append(remote(stat_in.at[pl.ds(4 * xd, 4)], stat_all.at[x], st_send.at[d], st_recv.at[d], dev))
                sends[-1].start()
            sends.append(remote(o_in.at[4 * xd + rows_of[k]], o_all.at[x, k], x_send.at[d, k], x_recv.at[d, k], dev))
            sends[-1].start()
    keep = [pltpu.make_async_copy(o_in.at[4 * x + rows_of[k]], o_all.at[x, k], own.at[k]) for k in range(4)]
    keep.append(pltpu.make_async_copy(stat_in.at[pl.ds(4 * x, 4)], stat_all.at[x], own.at[4]))
    for copy in keep:
        copy.start()

    def waiter(dst, recv):
        return remote(dst, dst, recv, recv, device(x, y, z, other))

    for copy in keep:
        copy.wait()
    for d in (1, 3, 2):
        waiter(stat_all.at[(x - d + NX) % NX], st_recv.at[d]).wait_recv()

    def columns(zd):
        return pl.ds(pl.multiple_of(group(zd) * SLAB, SLAB), SLAB)

    def local_of(k, cc):
        src = result.at[k, pl.ds(cc * HALF, HALF)]
        return pltpu.make_async_copy(src, out.at[:, columns(z)], own.at[5])

    def remote_of(k, cc):
        src = result.at[k, pl.ds(cc * HALF, HALF)]
        return remote(src, out.at[:, columns(z)], z_send.at[k, cc], z_recv.at[z],
                      device(x, y, 2 * rows_of[k] + c, cc))

    def deliver(k, act_local, act_remote):
        for cc in range(2):
            if shift[k]:
                act_remote(remote_of(k, cc))
                continue
            here = (z % 2 == c) & (c == cc)

            @pl.when(here)
            def _(cc=cc):
                act_local(local_of(k, cc))

            @pl.when(jnp.logical_not(here))
            def _(cc=cc):
                act_remote(remote_of(k, cc))

    def ship(k):
        deliver(k, lambda copy: copy.start(), lambda copy: copy.start())

    for k in range(4):
        for d in (1, 3, 2):
            waiter(o_all.at[(x - d + NX) % NX, k], x_recv.at[d, k]).wait_recv()
        for head in range(HEADS_HERE):
            m = [stat_all[s, rows_of[k], 2 * head:2 * head + 1, :] for s in range(NX)]
            top = jnp.maximum(jnp.maximum(m[0], m[1]), jnp.maximum(m[2], m[3]))
            w = [jnp.exp2(v - top) for v in m]
            total = sum(w[s] * stat_all[s, rows_of[k], 2 * head + 1:2 * head + 2, :] for s in range(NX))
            rows = slice(head * HEAD, (head + 1) * HEAD)
            share = 1.0 / total
            value = sum(o_all[s, k, rows, :].astype(jnp.float32) * (w[s] * share) for s in range(NX))
            result[k, :, rows] = value.T.astype(jnp.bfloat16)
        if k:
            ship(k - 1)
    ship(3)

    for zs in range(NZ):
        local = (zs == z) & (zs % 2 == c)

        @pl.when(jnp.logical_not(local))
        def _(zs=zs):
            waiter(out.at[:, columns(zs)], z_recv.at[zs]).wait_recv()
    for k in range(4):
        deliver(k, lambda copy: copy.wait(), lambda copy: copy.wait_send())
    for copy in sends:
        copy.wait_send()


def merge(partial, stats):
    any_space = pl.BlockSpec(memory_space=pl.ANY)
    dma = pltpu.SemaphoreType.DMA
    return pl.pallas_call(
        merge_kernel,
        out_shape=jax.ShapeDtypeStruct((HALF, NZ * SLAB), jnp.bfloat16),
        in_specs=[any_space, any_space],
        out_specs=any_space,
        scratch_shapes=[
            pltpu.VMEM((NX, 4, SLAB, BLOCK), jnp.bfloat16),
            pltpu.VMEM((NX, 4, 8, BLOCK), jnp.float32),
            pltpu.VMEM((4, BLOCK, SLAB), jnp.bfloat16),
            dma((NX, 4)), dma((NX, 4)), dma((NX,)), dma((NX,)),
            dma((4, 2)), dma((NZ,)), dma((6,)),
        ],
        compiler_params=pltpu.CompilerParams(
            collective_id=1, has_side_effects=True, vmem_limit_bytes=8 * 1024 * 1024),
        name="merge",
    )(partial, stats)


def per_device(queries, keys, values, block_mask, layout):
    kv, q, lists = gather(queries, keys, values, block_mask, layout)
    partial, stats = attend(lists, kv.reshape(KBLOCKS, BLOCK, 2 * SLAB), q.reshape(ITEMS, BLOCK, SLAB))
    return merge(partial, stats)


def solution(mesh):
    grid = Mesh(mesh.devices.reshape(NX, NY, 2, 4, 2), ("x", "y", "zh", "zl", "c"))
    rows = P(("x", "y", "zh", "zl", "c"), None)
    return jax.shard_map(
        per_device, mesh=grid,
        in_specs=(rows, rows, rows, P(("zl", "c"), None, None), P()),
        out_specs=rows, check_vma=False)
```
